32 devices in a mesh: pair: 4 (over y, x), virt: 8 (over z, core).
Axes of the slice: x: 2, y: 2, z: 4, core: 2. Of those that a mesh axis runs over, the one named last changes fastest.
Arguments:
- amplitudes: float32 [480, 12288], P('pair', 'virt'), may hold values from -6 to 6
- integrals: float32 [8192, 12288], P('pair', 'virt'), may hold values from -0.0546875 to 0.0546875
- eps_occ: float32 [120], replicated, may hold values from -2.5 to -0.3
- eps_vir: float32 [128], replicated, may hold values from 0.3 to 3
- pair_list: int32 [480, 2], P('pair'), may hold values from 0 to 119, as said below
Outputs:
- ladder: float32 [480, 8192], P('pair', 'virt')
- update: float32 [480, 8192], P('pair', 'virt')
The draws below stay inside these ranges and needn't reach their ends.
Inputs may be any that keep to these rules, and one draw needn't show every extreme that they name: `pair_list`: each row (i, j) has i < j; pairs may repeat.
All inputs are finite; a program needn't handle non-finite values.
Results may differ from the reference program's by a relative error of at most 0.000071.
Values sent between devices are 32-bit elements; how exact they have to be, the bound alone decides.
A program may use at most 64 MiB of HBM per device.

```python
import jax
import jax.numpy as jnp
from jax import lax

TILE = 64
NOCC = 120
PAIRS = 480
NVT = 128
AB = 8192
CD = 12288


def draw_pair_list(key, part):
    first_key, second_key, place_key = jax.random.split(jax.random.fold_in(key, 17), 3)
    smaller = jax.random.randint(first_key, (PAIRS,), 0, NOCC - 1)
    offsets = jax.random.randint(second_key, (PAIRS,), 0, 1 << 20)
    larger = smaller + 1 + offsets % (NOCC - 1 - smaller)
    where_full = jax.random.randint(place_key, (), 0, PAIRS)
    row_ids = jnp.arange(PAIRS)
    smaller = jnp.where(row_ids == where_full, 0, smaller)
    larger = jnp.where(row_ids == where_full, NOCC - 1, larger)
    return jnp.stack([smaller, larger], axis=1).astype(jnp.int32)


def level_of(stream_key, extent, cuts, least, high):
    def one(axis_at, shards_of):
        heights = jax.random.uniform(jax.random.fold_in(jax.random.fold_in(stream_key, 6), axis_at), (shards_of,), jnp.float32, least / len(cuts), high / len(cuts))
        return jnp.repeat(jnp.exp(heights), extent[axis_at] // shards_of).reshape((-1,) + (1,) * (len(extent) - axis_at - 1))

    gain = one(*cuts[0])
    for cut in cuts[1:]:
        gain = gain * one(*cut)
    return gain


def bell_draw(stream_key, extent, spread, most, pieces=(), dtype=jnp.bfloat16):
    array = jax.random.normal(stream_key, extent, jnp.float32) * spread
    if len(pieces) > 0:
        array = level_of(stream_key, extent, pieces, -0.22, 0.18) * array
    return jnp.clip(array, min=-most, max=most).astype(dtype)


def setup_inputs(seed: int = 0) -> dict:
    key_of = jax.random.split(jax.random.key(seed), 6)
    amplitudes = bell_draw(key_of[0], (PAIRS, CD), 1.0, 6.0, ((0, 4), (1, 8)), jnp.float32)
    integrals = bell_draw(key_of[1], (AB, CD), CD ** -0.5, 0.0546875, ((0, 4), (1, 8)), jnp.float32)
    eps_occ = jnp.clip(jax.random.uniform(key_of[2], (NOCC,), jnp.float32, -2.5, -0.3), -2.5, -0.3)
    eps_vir = jnp.clip(jax.random.uniform(key_of[3], (NVT,), jnp.float32, 0.3, 3.0), 0.3, 3.0)
    pair_list = draw_pair_list(jax.random.fold_in(key_of[5], 71), 0)
    return dict(amplitudes=amplitudes, integrals=integrals, eps_occ=eps_occ, eps_vir=eps_vir, pair_list=pair_list)


def reference(amplitudes, integrals, eps_occ, eps_vir, pair_list):
    ladder_raw = lax.dot_general(amplitudes, integrals, (((1,), (1,)), ((), ())), precision=lax.Precision.HIGHEST, preferred_element_type=jnp.float32)
    blocks = ladder_raw.reshape(PAIRS, 2, TILE, TILE)
    mirrored = jnp.swapaxes(blocks[:, ::-1], 2, 3)
    ladder = (blocks - mirrored).reshape(PAIRS, AB)
    pair_energy = eps_occ[pair_list[:, 0]] + eps_occ[pair_list[:, 1]]
    energy_tiles = eps_vir.reshape(2, TILE)
    virt_energy = (energy_tiles[:, :, None] + energy_tiles[::-1][:, None, :]).reshape(AB)
    update = ladder / (pair_energy[:, None] - virt_energy[None, :])
    return ladder, update
```

```python
import functools

import jax
import jax.numpy as jnp
from jax import lax
from jax.experimental import pallas as pl
from jax.experimental.pallas import tpu as pltpu
from jax.sharding import PartitionSpec as P

MESH = pl.DeviceIdType.MESH
LANES = 128


def antisymmetrize(partial_value, tile_width):
    blocks = partial_value.reshape(partial_value.shape[0], 2, tile_width, tile_width)
    mirrored = jnp.swapaxes(blocks[:, ::-1], 2, 3)
    return (blocks - mirrored).reshape(partial_value.shape)


def pair_energies(eps_occ, pair_list):
    occ_ids = lax.broadcasted_iota(jnp.int32, (1, 1, eps_occ.shape[0]), 2)
    one_hot = pair_list[:, :, None] == occ_ids
    return jnp.sum(jnp.where(one_hot, eps_occ[None, None, :], jnp.float32(0.0)), axis=(1, 2))


def sum_to_owners(antisym):
    return lax.psum_scatter(antisym, "virt", scatter_dimension=1, tiled=True)


def updated(ladder, eps_occ, eps_vir, pair_list):
    tile_width = eps_vir.shape[0] // 2
    column_count = ladder.shape[1]
    energy_tiles = eps_vir.reshape(2, tile_width)
    virt_energy = (energy_tiles[:, :, None] + energy_tiles[::-1][:, None, :]).reshape(
        2 * tile_width * tile_width
    )
    local_energy = lax.dynamic_slice_in_dim(
        virt_energy, lax.axis_index("virt") * column_count, column_count
    )
    pair_energy = pair_energies(eps_occ, pair_list)
    return ladder / (pair_energy[:, None] - local_energy[None, :])


def any_mesh_body(amplitudes, integrals, eps_occ, eps_vir, pair_list):
    tile_width = eps_vir.shape[0] // 2
    by_pairs = lax.dot_general(
        lax.all_gather(amplitudes, "pair", axis=0, tiled=True),
        integrals,
        (((1,), (1,)), ((), ())),
        precision=lax.Precision.HIGHEST,
        preferred_element_type=jnp.float32,
    )
    partial_value = lax.all_to_all(by_pairs, "pair", split_axis=0, concat_axis=1, tiled=True)
    ladder = sum_to_owners(antisymmetrize(partial_value, tile_width))
    return (ladder, updated(ladder, eps_occ, eps_vir, pair_list))


def split(value):
    high = value.astype(jnp.bfloat16)
    return high, (value - high.astype(jnp.float32)).astype(jnp.bfloat16)


def times(left, right):
    return lax.dot_general(
        left, right, (((1,), (1,)), ((), ())), preferred_element_type=jnp.float32
    )


def ladder_kernel(
    h, amp_ref, int_ref, out_ref, own, stage, int_high, int_low, blocks, weights, ct_ref,
    got, summed, rows, diff, below, above, upward, downward, kept, other, placed,
    own_sem, stage_sem, amp_send, amp_recv,
    core_send, core_recv, pair_send, pair_recv, up_send, up_recv, down_send, down_recv,
    last_send, last_recv,
):
    r = lax.axis_index("pair")
    v = lax.axis_index("virt")
    z = v // 2
    c = v % 2
    mate = v + 1 - 2 * c
    x = r % 2
    y = r // 2
    peers = (y * 2 + (1 - x), (1 - y) * 2 + x, (1 - y) * 2 + (1 - x))
    count, depth = own.shape
    third = depth // 3
    sizes = (third, third // 2, third, third // 2)
    starts = (0, third, third + third // 2, 2 * third + third // 2)
    step = stage.shape[1]
    steps = int_ref.shape[0] // step

    own_copy = pltpu.make_async_copy(amp_ref, own, own_sem)
    own_copy.start()

    def stage_copy(t):
        return pltpu.make_async_copy(
            int_ref.at[pl.ds(pl.multiple_of(t * step, 8), step)],
            stage.at[t % 2],
            stage_sem.at[t % 2],
        )

    stage_copy(0).start()
    stage_copy(1).start()

    barrier = pltpu.get_barrier_semaphore()
    pl.semaphore_signal(barrier, inc=1, device_id={"virt": mate}, device_id_type=MESH)
    for peer in peers:
        pl.semaphore_signal(barrier, inc=1, device_id={"pair": peer}, device_id_type=MESH)

    @pl.when(z < 3)
    def _():
        pl.semaphore_signal(barrier, inc=1, device_id={"virt": v + 2}, device_id_type=MESH)

    @pl.when(z > 0)
    def _():
        pl.semaphore_signal(barrier, inc=1, device_id={"virt": v - 2}, device_id_type=MESH)

    inner = jnp.logical_and(z > 0, z < 3)

    @pl.when(inner)
    def _():
        pl.semaphore_wait(barrier, 6)

    @pl.when(jnp.logical_not(inner))
    def _():
        pl.semaphore_wait(barrier, 5)

    def columns_of(part):
        return pl.ds(starts[part], sizes[part])

    def amp_copy(d, part):
        return pltpu.make_async_remote_copy(
            src_ref=amp_ref.at[:, columns_of(part)],
            dst_ref=blocks.at[d, :, columns_of(part)],
            send_sem=amp_send.at[d, part],
            recv_sem=amp_recv.at[d, part],
            device_id={"pair": peers[d]},
            device_id_type=MESH,
        )

    def pass_on(part):
        d = part // 2
        return pltpu.make_async_remote_copy(
            src_ref=blocks.at[d, :, columns_of(part)],
            dst_ref=blocks.at[2, :, columns_of(part)],
            send_sem=amp_send.at[2, part],
            recv_sem=amp_recv.at[2, part],
            device_id={"pair": peers[1 - d]},
            device_id_type=MESH,
        )

    for parts in zip((0, 1, 2, 3), (2, 0, 1, 3)):
        for d in range(2):
            amp_copy(d, parts[d]).start()

    def weigh(source, high_at, low_at, start, size):
        wide = 2 * LANES

        @pl.loop(0, size // wide)
        def _(k):
            columns = pl.ds(pl.multiple_of(start + k * wide, wide), wide)
            value = source[:, columns]
            if count < LANES:
                value = jnp.concatenate(
                    [value, jnp.zeros((LANES - count, wide), jnp.float32)], axis=0
                )
            high, low = split(value)
            weights[pl.ds(high_at * LANES, LANES), columns] = high
            weights[pl.ds(low_at * LANES, LANES), columns] = low

    def keep(t, size, lanes, value, first):
        per = size // (4 * h)
        i = t // (h // per)
        at = pl.multiple_of(t % (h // per) * per, per)
        place = (i, pl.ds(at, per), slice(None), slice(None), slice(None), lanes)
        value = value.reshape(per, 2, 2, h, value.shape[1])
        ct_ref[place] = value if first else ct_ref[place] + value

    def one_block(high, low, at, columns):
        both = times(high, weights[pl.ds(at * LANES, 2 * LANES), columns])
        rest = times(low, weights[pl.ds(at * LANES, LANES), columns])
        return both[:, :LANES] + both[:, LANES:] + rest

    own_copy.wait()
    weigh(own, 0, 1, 0, depth)

    @pl.loop(0, steps)
    def _(t):
        stage_copy(t).wait()
        high, low = split(stage[t % 2])
        at = pl.ds(pl.multiple_of(t * step, 16), step)
        int_high[at, :] = high
        int_low[at, :] = low

        @pl.when(t + 2 < steps)
        def _():
            stage_copy(t + 2).start()

        value = one_block(int_high[at, :], int_low[at, :], 0, slice(None))
        keep(t, step, pl.ds(3 * LANES, LANES), value, True)

    order = (peers[2], peers[0], peers[1], r)

    def core_copy(n, i):
        return pltpu.make_async_remote_copy(
            src_ref=ct_ref.at[i, :, :, (1 - c + i) % 2, :, pl.ds(n * LANES, LANES)],
            dst_ref=got.at[n, i],
            send_sem=core_send.at[n, i],
            recv_sem=core_recv.at[n, i],
            device_id={"virt": mate},
            device_id_type=MESH,
        )

    def pair_copy(n, piece, i):
        bh = (x if n == 2 else 1 - x) if piece == 0 else (1 - x if n == 2 else x)
        return pltpu.make_async_remote_copy(
            src_ref=summed.at[n, pl.ds(i * h, h), bh],
            dst_ref=rows.at[r, pl.ds(i * h, h), bh],
            send_sem=pair_send.at[n, piece, i],
            recv_sem=pair_recv.at[n, piece, i],
            device_id={"pair": order[n]},
            device_id_type=MESH,
        )

    def core_add(n, i):
        lanes = pl.ds(n * LANES, LANES)
        core_copy(n, i).wait_recv()

        @pl.loop(0, h, unroll=4)
        def _(a):
            for bh in range(2):
                total = ct_ref[i, a, bh, (c + i) % 2, :, lanes] + got[n, i, a, bh]
                if n < 3:
                    summed[n, i * h + a, bh] = total
                else:
                    rows[r, i * h + a, bh] = total

    big = 2 * step
    half = steps // 4

    def near_block(i, start, size, first):
        columns = pl.ds(start, size)

        @pl.loop(i * half, (i + 1) * half)
        def _(t):
            at = pl.ds(pl.multiple_of(t * big, 16), big)
            near_high = weights[pl.ds(4 * LANES, 2 * LANES), columns]
            near_low = weights[pl.ds(6 * LANES, 2 * LANES), columns]
            value = times(int_high[at, columns], near_high)
            value = value + times(int_high[at, columns], near_low)
            value = value + times(int_low[at, columns], near_high)
            keep(t, big, pl.ds(LANES, 2 * LANES), value, first)

    for i in range(2):
        core_copy(3, i).start()
    amp_copy(0, 0).wait_recv()
    pass_on(0).start()
    amp_copy(1, 2).wait_recv()
    pass_on(2).start()
    amp_copy(1, 0).wait_recv()
    for d in range(2):
        weigh(blocks.at[d], 4 + d, 6 + d, starts[0], sizes[0])
    for i in range(2):
        near_block(i, starts[0], sizes[0], True)
    amp_copy(0, 1).wait_recv()
    pass_on(1).start()
    for i in range(2):
        core_add(3, i)
    amp_copy(1, 1).wait_recv()
    amp_copy(0, 2).wait_recv()
    for d in range(2):
        weigh(blocks.at[d], 4 + d, 6 + d, starts[1], sizes[1] + sizes[2])
    for i in range(2):
        near_block(i, starts[1], sizes[1] + sizes[2], False)
    amp_copy(1, 3).wait_recv()
    pass_on(3).start()
    amp_copy(0, 3).wait_recv()
    for d in range(2):
        weigh(blocks.at[d], 4 + d, 6 + d, starts[3], sizes[3])
    for i in range(2):
        near_block(i, starts[3], sizes[3], False)
        core_copy(2, i).start()
        core_copy(1, i).start()
    for i in range(2):
        core_add(2, i)
        pair_copy(2, 0, i).start()
        core_add(1, i)
        pair_copy(1, 0, i).start()
    for n in (2, 1):
        for i in range(2):
            pair_copy(n, 1, i).start()

    def far_block(i, parts, first):
        @pl.loop(i * half, (i + 1) * half)
        def _(t):
            at = pl.ds(pl.multiple_of(t * big, 16), big)
            values = [
                one_block(int_high[at, columns_of(p)], int_low[at, columns_of(p)], 2, columns_of(p))
                for p in parts
            ]
            keep(t, big, pl.ds(0, LANES), values[0] + values[1], first)

    for parts in ((0, 2), (1, 3)):
        for p in parts:
            pass_on(p).wait_recv()
            weigh(blocks.at[2], 2, 3, starts[p], sizes[p])
        for i in range(2):
            far_block(i, parts, parts[0] == 0)
            if parts[0] == 1:
                core_copy(0, i).start()

    def antisym(q, i, u):
        ah = q // 2
        bh = q % 2
        mirror = (c + i) % 2

        @pl.loop(0, h // 2, unroll=4)
        def _(n):
            a = u * (h // 2) + n
            plain = rows[ah, i * h + a, bh]
            turned = rows[2 + bh, pl.ds(mirror * h, h), ah, a, :]
            diff[q * 4 + i * 2 + u, pl.ds(pl.multiple_of(n * h, 8), h), :] = plain - turned

    def up_copy(q):
        return pltpu.make_async_remote_copy(
            src_ref=upward.at[q], dst_ref=below.at[q],
            send_sem=up_send.at[q], recv_sem=up_recv.at[q],
            device_id={"virt": v + 2}, device_id_type=MESH,
        )

    def down_copy(q):
        return pltpu.make_async_remote_copy(
            src_ref=downward.at[q], dst_ref=above.at[q],
            send_sem=down_send.at[q], recv_sem=down_recv.at[q],
            device_id={"virt": v - 2}, device_id_type=MESH,
        )

    def sends_up(q):
        return jnp.logical_or(z < 2, jnp.logical_and(z == 2, q // 4 % 2 == 1))

    def sends_down(q):
        return jnp.logical_or(z > 1, jnp.logical_and(z == 1, q // 8 == 0))

    def hears_below(q):
        return jnp.logical_or(inner, jnp.logical_and(z == 3, q // 4 % 2 == 1))

    def hears_above(q):
        return jnp.logical_or(inner, jnp.logical_and(z == 0, q // 8 == 0))

    def go_up(q):
        @pl.when(hears_below(q))
        def _():
            up_copy(q).wait_recv()

        @pl.when(z == 0)
        def _():
            upward[q] = diff[q]

        @pl.when(jnp.logical_and(z > 0, sends_up(q)))
        def _():
            upward[q] = diff[q] + below[q]

        @pl.when(sends_up(q))
        def _():
            up_copy(q).start()

    def go_down(q):
        @pl.when(hears_above(q))
        def _():
            down_copy(q).wait_recv()

        @pl.when(z == 3)
        def _():
            downward[q] = diff[q]

        @pl.when(jnp.logical_and(z < 3, sends_down(q)))
        def _():
            downward[q] = diff[q] + above[q]

        @pl.when(sends_down(q))
        def _():
            down_copy(q).start()

    def near(q):
        @pl.when(z < 2)
        def _():
            go_up(q)

        @pl.when(z >= 2)
        def _():
            go_down(q)

    def far(q):
        @pl.when(z < 2)
        def _():
            go_down(q)

        @pl.when(z >= 2)
        def _():
            go_up(q)

    alike = x * 3
    unlike = (1 - x) * 3
    mixed_near = jnp.where(y == 0, unlike // 3 * 2 + x, x * 2 + 1 - x)
    mixed_far = jnp.where(y == 0, x * 2 + 1 - x, (1 - x) * 2 + x)
    quads = (alike, mixed_near, mixed_far, unlike)
    turns = [jnp.where(y == 0, (t + c) % 2, t) for t in range(2)]
    chunks = [q * 4 + turns[t] * 2 + u for q in quads for t in range(2) for u in range(2)]
    needs = (
        ((2, 0, 0),), ((2, 0, 1),),
        ((1, 0, 0), (1, 0, 1), (2, 1, 0)), ((2, 1, 1),),
        ((0, 0, 0),), ((0, 0, 1),),
        ((1, 1, 0), (1, 1, 1), (0, 1, 0)), ((0, 1, 1),),
    )
    lag = 3
    for s in range(16):
        if s % 2 == 0:
            for n, piece, i in needs[s // 2]:
                pair_copy(n, piece, i).wait_recv()
        antisym(quads[s // 4], turns[s // 2 % 2], s % 2)
        near(chunks[s])
        if s == 1:
            for i in range(2):
                core_add(0, i)
            for piece in range(2):
                for i in range(2):
                    pair_copy(0, piece, i).start()
        if s >= lag:

            @pl.when(inner)
            def _():
                far(chunks[s - lag])

    @pl.when(jnp.logical_not(inner))
    def _():
        for s in range(16 - lag):
            far(chunks[s])

    for s in range(16 - lag, 16):
        far(chunks[s])

    def total_of(t, i):
        q = pl.ds(jnp.where(z < 2, z * 2 + t, t * 2 + z - 2) * 4 + i * 2, 2)
        low = jnp.where(z > 0, below[q], jnp.float32(0.0))
        high = jnp.where(z < 3, above[q], jnp.float32(0.0))
        return (diff[q] + low + high).reshape(h * h, LANES)

    mine = jnp.where(z < 2, c, 0)

    def last_copy(t):
        return pltpu.make_async_remote_copy(
            src_ref=other.at[t], dst_ref=kept.at[1, t],
            send_sem=last_send.at[t], recv_sem=last_recv.at[t],
            device_id={"virt": mate}, device_id_type=MESH,
        )

    for t in range(2):
        other[t] = total_of(t, jnp.where(z < 2, 1 - c, 1))
        last_copy(t).start()
    for t in range(2):
        kept[0, t] = total_of(t, mine)

    def put(s, t):
        @pl.loop(0, h, unroll=4)
        def _(a):
            at = pl.multiple_of((a * 4 + 2 * t + s) * h, 8)
            plain = kept[s, t, pl.ds(pl.multiple_of(a * h, 8), h), :]
            turned = kept[s, t, pl.ds(a, h, stride=h), :]
            placed[pl.ds(at, h), :] = jnp.where(z < 2, plain, turned)

    for t in range(2):
        put(0, t)
    for t in range(2):
        last_copy(t).wait_recv()
        put(1, t)

    for n in range(out_ref.shape[1] // LANES):
        at = pl.ds(n * LANES, LANES)
        out_ref[:, at] = placed[at, :].T[:count]

    for t in range(2):
        last_copy(t).wait_send()
    for part in range(4):
        for d in range(2):
            amp_copy(d, part).wait_send()
        pass_on(part).wait_send()
    for n in range(4):
        for i in range(2):
            core_copy(n, i).wait_send()
    for n in range(3):
        for piece in range(2):
            for i in range(2):
                pair_copy(n, piece, i).wait_send()
    for q in range(16):

        @pl.when(sends_up(q))
        def _():
            up_copy(q).wait_send()

        @pl.when(sends_down(q))
        def _():
            down_copy(q).wait_send()


def ladder_of(amplitudes, integrals, tile_width):
    h = tile_width // 4
    count, depth = amplitudes.shape
    owned = integrals.shape[0]
    step = owned // 8
    f32 = jnp.float32
    bf16 = jnp.bfloat16
    dma = pltpu.SemaphoreType.DMA
    return pl.pallas_call(
        functools.partial(ladder_kernel, h),
        out_shape=pltpu.VMEM((count, tile_width * h), f32),
        in_specs=[pl.BlockSpec(memory_space=pl.ANY), pl.BlockSpec(memory_space=pl.ANY)],
        out_specs=pl.BlockSpec(memory_space=pltpu.VMEM),
        scratch_shapes=[
            pltpu.VMEM((count, depth), f32),
            pltpu.VMEM((2, step, depth), f32),
            pltpu.VMEM((owned, depth), bf16),
            pltpu.VMEM((owned, depth), bf16),
            pltpu.VMEM((3, count, depth), f32),
            pltpu.VMEM((8 * LANES, depth), bf16),
            pltpu.VMEM((2, h, 2, 2, h, 4 * LANES), f32),
            pltpu.VMEM((4, 2, h, 2, h, LANES), f32),
            pltpu.VMEM((3, 2 * h, 2, h, LANES), f32),
            pltpu.VMEM((4, 2 * h, 2, h, LANES), f32),
            pltpu.VMEM((16, h * h // 2, LANES), f32),
            pltpu.VMEM((16, h * h // 2, LANES), f32),
            pltpu.VMEM((16, h * h // 2, LANES), f32),
            pltpu.VMEM((16, h * h // 2, LANES), f32),
            pltpu.VMEM((16, h * h // 2, LANES), f32),
            pltpu.VMEM((2, 2, h * h, LANES), f32),
            pltpu.VMEM((2, h * h, LANES), f32),
            pltpu.VMEM((tile_width * h, LANES), f32),
            dma, dma((2,)), dma((3, 4)), dma((3, 4)),
            dma((4, 2)), dma((4, 2)), dma((3, 2, 2)), dma((3, 2, 2)),
            dma((16,)), dma((16,)), dma((16,)), dma((16,)), dma((2,)), dma((2,)),
        ],
        compiler_params=pltpu.CompilerParams(
            collective_id=0, has_side_effects=True, vmem_limit_bytes=58 * 1024 * 1024
        ),
        name="ladder",
    )(amplitudes, integrals)


def block_body(amplitudes, integrals, eps_occ, eps_vir, pair_list):
    tile_width = eps_vir.shape[0] // 2
    first = lax.axis_index("virt") < lax.axis_size("virt") // 2
    sign = jnp.where(first, jnp.float32(1.0), jnp.float32(-1.0))
    raw = ladder_of(amplitudes, integrals, tile_width)
    raw, eps_occ, eps_vir, pair_list = lax.optimization_barrier(
        (raw, eps_occ, eps_vir, pair_list)
    )
    ladder = sign * raw
    return (ladder, updated(ladder, eps_occ, eps_vir, pair_list))


def solution(mesh):
    in_specs = (P("pair", "virt"), P("pair", "virt"), P(), P(), P("pair", None))
    out_specs = (P("pair", "virt"), P("pair", "virt"))
    fits = mesh.shape["pair"] == 4 and mesh.shape["virt"] == 8

    def body(amplitudes, integrals, eps_occ, eps_vir, pair_list):
        tiled = eps_vir.shape[0] % 64 == 0 and amplitudes.shape[0] <= LANES
        tiled = tiled and amplitudes.shape[1] % (12 * LANES) == 0
        chosen = block_body if fits and tiled else any_mesh_body
        return chosen(amplitudes, integrals, eps_occ, eps_vir, pair_list)

    return jax.shard_map(body, mesh=mesh, in_specs=in_specs, out_specs=out_specs, check_vma=False)
```

```python
import functools

import jax
import jax.numpy as jnp
from jax import lax
from jax.experimental import pallas as pl
from jax.experimental.pallas import tpu as pltpu
from jax.sharding import PartitionSpec as P

MESH = pl.DeviceIdType.MESH
LANES = 128


def antisymmetrize(partial_value, tile_width):
    blocks = partial_value.reshape(partial_value.shape[0], 2, tile_width, tile_width)
    mirrored = jnp.swapaxes(blocks[:, ::-1], 2, 3)
    return (blocks - mirrored).reshape(partial_value.shape)


def pair_energies(eps_occ, pair_list):
    occ_ids = lax.broadcasted_iota(jnp.int32, (1, 1, eps_occ.shape[0]), 2)
    one_hot = pair_list[:, :, None] == occ_ids
    return jnp.sum(jnp.where(one_hot, eps_occ[None, None, :], jnp.float32(0.0)), axis=(1, 2))


def sum_to_owners(antisym):
    return lax.psum_scatter(antisym, "virt", scatter_dimension=1, tiled=True)


def updated(ladder, eps_occ, eps_vir, pair_list):
    tile_width = eps_vir.shape[0] // 2
    column_count = ladder.shape[1]
    energy_tiles = eps_vir.reshape(2, tile_width)
    virt_energy = (energy_tiles[:, :, None] + energy_tiles[::-1][:, None, :]).reshape(
        2 * tile_width * tile_width
    )
    local_energy = lax.dynamic_slice_in_dim(
        virt_energy, lax.axis_index("virt") * column_count, column_count
    )
    pair_energy = pair_energies(eps_occ, pair_list)
    return ladder / (pair_energy[:, None] - local_energy[None, :])


def any_mesh_body(amplitudes, integrals, eps_occ, eps_vir, pair_list):
    tile_width = eps_vir.shape[0] // 2
    by_pairs = lax.dot_general(
        lax.all_gather(amplitudes, "pair", axis=0, tiled=True),
        integrals,
        (((1,), (1,)), ((), ())),
        precision=lax.Precision.HIGHEST,
        preferred_element_type=jnp.float32,
    )
    partial_value = lax.all_to_all(by_pairs, "pair", split_axis=0, concat_axis=1, tiled=True)
    ladder = sum_to_owners(antisymmetrize(partial_value, tile_width))
    return (ladder, updated(ladder, eps_occ, eps_vir, pair_list))


def split(value):
    high = value.astype(jnp.bfloat16)
    return high, (value - high.astype(jnp.float32)).astype(jnp.bfloat16)


def times(left, right):
    return lax.dot_general(
        left, right, (((1,), (1,)), ((), ())), preferred_element_type=jnp.float32
    )


def ladder_kernel(
    h, amp_ref, int_ref, out_ref, own, stage, int_high, int_low, blocks, weights, ct_ref,
    got, summed, rows, diff, below, above, sums, kept, other, placed,
    own_sem, stage_sem, amp_send, amp_recv,
    core_send, core_recv, pair_send, pair_recv,
    main_send, side_send, below_recv, above_recv, last_send, last_recv,
):
    r = lax.axis_index("pair")
    v = lax.axis_index("virt")
    z = v // 2
    c = v % 2
    mate = v + 1 - 2 * c
    x = r % 2
    y = r // 2
    peers = (y * 2 + (1 - x), (1 - y) * 2 + x, (1 - y) * 2 + (1 - x))
    count, depth = own.shape
    third = depth // 3
    sizes = (third, third // 2, third, third // 2)
    starts = (0, third, third + third // 2, 2 * third + third // 2)
    step = stage.shape[1]
    steps = int_ref.shape[0] // step

    own_copy = pltpu.make_async_copy(amp_ref, own, own_sem)
    own_copy.start()

    def stage_copy(t):
        return pltpu.make_async_copy(
            int_ref.at[pl.ds(pl.multiple_of(t * step, 8), step)],
            stage.at[t % 2],
            stage_sem.at[t % 2],
        )

    stage_copy(0).start()
    stage_copy(1).start()

    barrier = pltpu.get_barrier_semaphore()
    pl.semaphore_signal(barrier, inc=1, device_id={"virt": mate}, device_id_type=MESH)
    for peer in peers:
        pl.semaphore_signal(barrier, inc=1, device_id={"pair": peer}, device_id_type=MESH)

    @pl.when(z < 3)
    def _():
        pl.semaphore_signal(barrier, inc=1, device_id={"virt": v + 2}, device_id_type=MESH)

    @pl.when(z > 0)
    def _():
        pl.semaphore_signal(barrier, inc=1, device_id={"virt": v - 2}, device_id_type=MESH)

    across = (v + 4) % 8
    pl.semaphore_signal(barrier, inc=1, device_id={"virt": across}, device_id_type=MESH)
    inner = jnp.logical_and(z > 0, z < 3)

    @pl.when(inner)
    def _():
        pl.semaphore_wait(barrier, 7)

    @pl.when(jnp.logical_not(inner))
    def _():
        pl.semaphore_wait(barrier, 6)

    def columns_of(part):
        return pl.ds(starts[part], sizes[part])

    def amp_copy(d, part):
        return pltpu.make_async_remote_copy(
            src_ref=amp_ref.at[:, columns_of(part)],
            dst_ref=blocks.at[d, :, columns_of(part)],
            send_sem=amp_send.at[d, part],
            recv_sem=amp_recv.at[d, part],
            device_id={"pair": peers[d]},
            device_id_type=MESH,
        )

    def pass_on(part):
        d = part // 2
        return pltpu.make_async_remote_copy(
            src_ref=blocks.at[d, :, columns_of(part)],
            dst_ref=blocks.at[2, :, columns_of(part)],
            send_sem=amp_send.at[2, part],
            recv_sem=amp_recv.at[2, part],
            device_id={"pair": peers[1 - d]},
            device_id_type=MESH,
        )

    for parts in zip((0, 1, 2, 3), (2, 0, 1, 3)):
        for d in range(2):
            amp_copy(d, parts[d]).start()

    def weigh(source, high_at, low_at, start, size):
        wide = 2 * LANES

        @pl.loop(0, size // wide)
        def _(k):
            columns = pl.ds(pl.multiple_of(start + k * wide, wide), wide)
            value = source[:, columns]
            if count < LANES:
                value = jnp.concatenate(
                    [value, jnp.zeros((LANES - count, wide), jnp.float32)], axis=0
                )
            high, low = split(value)
            weights[pl.ds(high_at * LANES, LANES), columns] = high
            weights[pl.ds(low_at * LANES, LANES), columns] = low

    def keep(t, size, lanes, value, first):
        per = size // (4 * h)
        i = t // (h // per)
        at = pl.multiple_of(t % (h // per) * per, per)
        place = (i, pl.ds(at, per), slice(None), slice(None), slice(None), lanes)
        value = value.reshape(per, 2, 2, h, value.shape[1])
        ct_ref[place] = value if first else ct_ref[place] + value

    def one_block(high, low, at, columns):
        both = times(high, weights[pl.ds(at * LANES, 2 * LANES), columns])
        rest = times(low, weights[pl.ds(at * LANES, LANES), columns])
        return both[:, :LANES] + both[:, LANES:] + rest

    own_copy.wait()
    weigh(own, 0, 1, 0, depth)

    @pl.loop(0, steps)
    def _(t):
        stage_copy(t).wait()
        high, low = split(stage[t % 2])
        at = pl.ds(pl.multiple_of(t * step, 16), step)
        int_high[at, :] = high
        int_low[at, :] = low

        @pl.when(t + 2 < steps)
        def _():
            stage_copy(t + 2).start()

        value = one_block(int_high[at, :], int_low[at, :], 0, slice(None))
        keep(t, step, pl.ds(3 * LANES, LANES), value, True)

    order = (peers[2], peers[0], peers[1], r)

    def core_copy(n, i):
        return pltpu.make_async_remote_copy(
            src_ref=ct_ref.at[i, :, :, (1 - c + i) % 2, :, pl.ds(n * LANES, LANES)],
            dst_ref=got.at[n, i],
            send_sem=core_send.at[n, i],
            recv_sem=core_recv.at[n, i],
            device_id={"virt": mate},
            device_id_type=MESH,
        )

    def pair_copy(n, piece, i):
        bh = (x if n == 2 else 1 - x) if piece == 0 else (1 - x if n == 2 else x)
        return pltpu.make_async_remote_copy(
            src_ref=summed.at[n, pl.ds(i * h, h), bh],
            dst_ref=rows.at[r, pl.ds(i * h, h), bh],
            send_sem=pair_send.at[n, piece, i],
            recv_sem=pair_recv.at[n, piece, i],
            device_id={"pair": order[n]},
            device_id_type=MESH,
        )

    def core_add(n, i):
        lanes = pl.ds(n * LANES, LANES)
        core_copy(n, i).wait_recv()

        @pl.loop(0, h, unroll=4)
        def _(a):
            for bh in range(2):
                total = ct_ref[i, a, bh, (c + i) % 2, :, lanes] + got[n, i, a, bh]
                if n < 3:
                    summed[n, i * h + a, bh] = total
                else:
                    rows[r, i * h + a, bh] = total

    big = 2 * step
    half = steps // 4

    def near_block(i, start, size, first):
        columns = pl.ds(start, size)

        @pl.loop(i * half, (i + 1) * half)
        def _(t):
            at = pl.ds(pl.multiple_of(t * big, 16), big)
            near_high = weights[pl.ds(4 * LANES, 2 * LANES), columns]
            near_low = weights[pl.ds(6 * LANES, 2 * LANES), columns]
            value = times(int_high[at, columns], near_high)
            value = value + times(int_high[at, columns], near_low)
            value = value + times(int_low[at, columns], near_high)
            keep(t, big, pl.ds(LANES, 2 * LANES), value, first)

    for i in range(2):
        core_copy(3, i).start()
    amp_copy(0, 0).wait_recv()
    pass_on(0).start()
    amp_copy(1, 2).wait_recv()
    pass_on(2).start()
    amp_copy(1, 0).wait_recv()
    for d in range(2):
        weigh(blocks.at[d], 4 + d, 6 + d, starts[0], sizes[0])
    for i in range(2):
        near_block(i, starts[0], sizes[0], True)
    amp_copy(0, 1).wait_recv()
    pass_on(1).start()
    for i in range(2):
        core_add(3, i)
    amp_copy(1, 1).wait_recv()
    amp_copy(0, 2).wait_recv()
    for d in range(2):
        weigh(blocks.at[d], 4 + d, 6 + d, starts[1], sizes[1] + sizes[2])
    for i in range(2):
        near_block(i, starts[1], sizes[1] + sizes[2], False)
    amp_copy(1, 3).wait_recv()
    pass_on(3).start()
    amp_copy(0, 3).wait_recv()
    for d in range(2):
        weigh(blocks.at[d], 4 + d, 6 + d, starts[3], sizes[3])
    for i in range(2):
        near_block(i, starts[3], sizes[3], False)
        core_copy(2, i).start()
        core_copy(1, i).start()
    for i in range(2):
        core_add(2, i)
        pair_copy(2, 0, i).start()
        core_add(1, i)
        pair_copy(1, 0, i).start()
    for n in (2, 1):
        for i in range(2):
            pair_copy(n, 1, i).start()

    def far_block(i, parts, first):
        @pl.loop(i * half, (i + 1) * half)
        def _(t):
            at = pl.ds(pl.multiple_of(t * big, 16), big)
            values = [
                one_block(int_high[at, columns_of(p)], int_low[at, columns_of(p)], 2, columns_of(p))
                for p in parts
            ]
            keep(t, big, pl.ds(0, LANES), values[0] + values[1], first)

    for parts in ((0, 2), (1, 3)):
        for p in parts:
            pass_on(p).wait_recv()
            weigh(blocks.at[2], 2, 3, starts[p], sizes[p])
        for i in range(2):
            far_block(i, parts, parts[0] == 0)
            if parts[0] == 1:
                core_copy(0, i).start()

    def antisym(q, i, u, size):
        ah = q // 2
        bh = q % 2
        mirror = (c + i) % 2
        rises = h // 4

        @pl.loop(0, size * rises, unroll=4)
        def _(n):
            a = u * rises + n
            plain = rows[ah, i * h + a, bh]
            turned = rows[2 + bh, pl.ds(mirror * h, h), ah, a, :]
            at = q * 8 + i * 4 + u + n // rises
            diff[at, pl.ds(pl.multiple_of(n % rises * h, 8), h), :] = plain - turned

    def main_copy(upwards, q, k, size):
        far_up = jnp.where(z == 0, 0, q % 2)
        far_down = jnp.where(z == 3, 0, 1 - q // 2)
        at = pl.ds(k, size)
        return pltpu.make_async_remote_copy(
            src_ref=sums.at[at],
            dst_ref=(below if upwards else above).at[at],
            send_sem=main_send.at[k],
            recv_sem=(below_recv if upwards else above_recv).at[k],
            device_id={"virt": v + 2 + 2 * far_up if upwards else v - 2 - 2 * far_down},
            device_id_type=MESH,
        )

    def side_copy(upwards, k, size):
        at = pl.ds(k, size)
        return pltpu.make_async_remote_copy(
            src_ref=diff.at[at],
            dst_ref=(above if upwards else below).at[at],
            send_sem=side_send.at[k],
            recv_sem=(above_recv if upwards else below_recv).at[k],
            device_id={"virt": v + 2 if upwards else v - 2},
            device_id_type=MESH,
        )

    def side_down(q):
        return jnp.logical_and(z == 1, q // 2 == 0)

    def side_up(q):
        return jnp.logical_and(z == 2, q % 2 == 1)

    def near(q, k, size):
        at = pl.ds(k, size)

        @pl.when(side_down(q))
        def _():
            side_copy(False, k, size).start()

        @pl.when(side_up(q))
        def _():
            side_copy(True, k, size).start()

        @pl.when(jnp.logical_not(inner))
        def _():
            sums[at] = diff[at]

        @pl.when(z == 1)
        def _():
            main_copy(True, q, k, size).wait_recv()
            sums[at] = diff[at] + below[at]

        @pl.when(z == 2)
        def _():
            main_copy(False, q, k, size).wait_recv()
            sums[at] = diff[at] + above[at]

        @pl.when(z < 2)
        def _():
            main_copy(True, q, k, size).start()

        @pl.when(z >= 2)
        def _():
            main_copy(False, q, k, size).start()

    def last_copy(t, u, size):
        at = pl.ds(pl.multiple_of(u * piece_rows, 8), size * piece_rows)
        return pltpu.make_async_remote_copy(
            src_ref=other.at[t, at],
            dst_ref=kept.at[1, t, at],
            send_sem=last_send.at[t, u],
            recv_sem=last_recv.at[t, u],
            device_id={"virt": mate},
            device_id_type=MESH,
        )

    piece_rows = h * h // 4
    ours = jnp.where(z < 2, c, 0)

    def owned_here(q):
        return jnp.where(z < 2, q // 2 == z, q % 2 == z - 2)

    def place_of(q):
        return jnp.where(z < 2, q % 2, q // 2)

    def finish(q, i, u, size):
        k = q * 8 + i * 4 + u
        at = pl.ds(k, size)
        t = place_of(q)
        to = pl.ds(pl.multiple_of(u * piece_rows, 8), size * piece_rows)

        @pl.when(owned_here(q))
        def _():
            @pl.when(z != 1)
            def _():
                main_copy(True, q, k, size).wait_recv()

            @pl.when(z != 2)
            def _():
                main_copy(False, q, k, size).wait_recv()

            total = (diff[at] + below[at] + above[at]).reshape(size * piece_rows, LANES)

            @pl.when(i == ours)
            def _():
                kept[0, t, to] = total

            @pl.when(i != ours)
            def _():
                other[t, to] = total
                last_copy(t, u, size).start()

    alike = x * 3
    unlike = (1 - x) * 3
    mixed_near = jnp.where(y == 0, (1 - x) * 2 + x, x * 2 + 1 - x)
    mixed_far = jnp.where(y == 0, x * 2 + 1 - x, (1 - x) * 2 + x)
    quads = (alike, mixed_near, mixed_far, unlike)
    turns = [jnp.where(y == 0, (t + c) % 2, t) for t in range(2)]
    mate_turns = [jnp.where(y == 0, (t + 1 - c) % 2, t) for t in range(2)]
    mate_ours = jnp.where(z < 2, 1 - c, 0)
    needs = (
        ((2, 0, 0),), ((2, 0, 1),),
        ((1, 0, 0), (1, 0, 1), (2, 1, 0)), ((2, 1, 1),),
        ((0, 0, 0),), ((0, 0, 1),),
        ((1, 1, 0), (1, 1, 1), (0, 1, 0)), ((0, 1, 1),),
    )
    todo = []
    for g in range(4):
        for t in range(2):
            size = 1 if g == 3 else 2
            for u in range(0, 4, size):
                todo.append((g, t, u, size))
    lag = 6
    for s, (g, t, u, size) in enumerate(todo):
        q = quads[g]
        if u == 0:
            for n, piece, i in needs[g * 2 + t]:
                pair_copy(n, piece, i).wait_recv()
        antisym(q, turns[t], u, size)
        near(q, q * 8 + turns[t] * 4 + u, size)
        if s == 1:
            for i in range(2):
                core_add(0, i)
            for piece in range(2):
                for i in range(2):
                    pair_copy(0, piece, i).start()
        if s >= lag:
            eg, et, eu, esize = todo[s - lag]

            @pl.when(inner)
            def _():
                finish(quads[eg], turns[et], eu, esize)

    @pl.when(jnp.logical_not(inner))
    def _():
        for g, t, u, size in todo[: len(todo) - lag]:
            finish(quads[g], turns[t], u, size)

    for g, t, u, size in todo[len(todo) - lag :]:
        finish(quads[g], turns[t], u, size)

    def put(s, t):
        @pl.loop(0, h, unroll=4)
        def _(a):
            at = pl.multiple_of((a * 4 + 2 * t + s) * h, 8)
            plain = kept[s, t, pl.ds(pl.multiple_of(a * h, 8), h), :]
            turned = kept[s, t, pl.ds(a, h, stride=h), :]
            placed[pl.ds(at, h), :] = jnp.where(z < 2, plain, turned)

    for t in range(2):
        put(0, t)
    for g, t, u, size in todo:
        q = quads[g]

        @pl.when(jnp.logical_and(owned_here(q), mate_turns[t] != mate_ours))
        def _():
            last_copy(place_of(q), u, size).wait_recv()

    for t in range(2):
        put(1, t)

    for n in range(out_ref.shape[1] // LANES):
        at = pl.ds(n * LANES, LANES)
        out_ref[:, at] = placed[at, :].T[:count]

    for part in range(4):
        for d in range(2):
            amp_copy(d, part).wait_send()
        pass_on(part).wait_send()
    for n in range(4):
        for i in range(2):
            core_copy(n, i).wait_send()
    for n in range(3):
        for piece in range(2):
            for i in range(2):
                pair_copy(n, piece, i).wait_send()
    for g, t, u, size in todo:
        q = quads[g]
        k = q * 8 + turns[t] * 4 + u
        main_copy(True, q, k, size).wait_send()

        @pl.when(jnp.logical_or(side_down(q), side_up(q)))
        def _():
            side_copy(True, k, size).wait_send()

        @pl.when(jnp.logical_and(owned_here(q), turns[t] != ours))
        def _():
            last_copy(place_of(q), u, size).wait_send()


def ladder_of(amplitudes, integrals, tile_width):
    h = tile_width // 4
    count, depth = amplitudes.shape
    owned = integrals.shape[0]
    step = owned // 8
    f32 = jnp.float32
    bf16 = jnp.bfloat16
    dma = pltpu.SemaphoreType.DMA
    return pl.pallas_call(
        functools.partial(ladder_kernel, h),
        out_shape=pltpu.VMEM((count, tile_width * h), f32),
        in_specs=[pl.BlockSpec(memory_space=pl.ANY), pl.BlockSpec(memory_space=pl.ANY)],
        out_specs=pl.BlockSpec(memory_space=pltpu.VMEM),
        scratch_shapes=[
            pltpu.VMEM((count, depth), f32),
            pltpu.VMEM((2, step, depth), f32),
            pltpu.VMEM((owned, depth), bf16),
            pltpu.VMEM((owned, depth), bf16),
            pltpu.VMEM((3, count, depth), f32),
            pltpu.VMEM((8 * LANES, depth), bf16),
            pltpu.VMEM((2, h, 2, 2, h, 4 * LANES), f32),
            pltpu.VMEM((4, 2, h, 2, h, LANES), f32),
            pltpu.VMEM((3, 2 * h, 2, h, LANES), f32),
            pltpu.VMEM((4, 2 * h, 2, h, LANES), f32),
            pltpu.VMEM((32, h * h // 4, LANES), f32),
            pltpu.VMEM((32, h * h // 4, LANES), f32),
            pltpu.VMEM((32, h * h // 4, LANES), f32),
            pltpu.VMEM((32, h * h // 4, LANES), f32),
            pltpu.VMEM((2, 2, h * h, LANES), f32),
            pltpu.VMEM((2, h * h, LANES), f32),
            pltpu.VMEM((tile_width * h, LANES), f32),
            dma, dma((2,)), dma((3, 4)), dma((3, 4)),
            dma((4, 2)), dma((4, 2)), dma((3, 2, 2)), dma((3, 2, 2)),
            dma((32,)), dma((32,)), dma((32,)), dma((32,)), dma((2, 4)), dma((2, 4)),
        ],
        compiler_params=pltpu.CompilerParams(
            collective_id=0, has_side_effects=True, vmem_limit_bytes=58 * 1024 * 1024
        ),
        name="ladder",
    )(amplitudes, integrals)


def block_body(amplitudes, integrals, eps_occ, eps_vir, pair_list):
    tile_width = eps_vir.shape[0] // 2
    first = lax.axis_index("virt") < lax.axis_size("virt") // 2
    sign = jnp.where(first, jnp.float32(1.0), jnp.float32(-1.0))
    raw = ladder_of(amplitudes, integrals, tile_width)
    raw, eps_occ, eps_vir, pair_list = lax.optimization_barrier(
        (raw, eps_occ, eps_vir, pair_list)
    )
    ladder = sign * raw
    return (ladder, updated(ladder, eps_occ, eps_vir, pair_list))


def solution(mesh):
    in_specs = (P("pair", "virt"), P("pair", "virt"), P(), P(), P("pair", None))
    out_specs = (P("pair", "virt"), P("pair", "virt"))
    fits = mesh.shape["pair"] == 4 and mesh.shape["virt"] == 8

    def body(amplitudes, integrals, eps_occ, eps_vir, pair_list):
        tiled = eps_vir.shape[0] % 64 == 0 and amplitudes.shape[0] <= LANES
        tiled = tiled and amplitudes.shape[1] % (12 * LANES) == 0
        chosen = block_body if fits and tiled else any_mesh_body
        return chosen(amplitudes, integrals, eps_occ, eps_vir, pair_list)

    return jax.shard_map(body, mesh=mesh, in_specs=in_specs, out_specs=out_specs, check_vma=False)
```

```python
import functools

import jax
import jax.numpy as jnp
from jax import lax
from jax.experimental import pallas as pl
from jax.experimental.pallas import tpu as pltpu
from jax.sharding import PartitionSpec as P

MESH = pl.DeviceIdType.MESH
LANES = 128


def antisymmetrize(partial_value, tile_width):
    blocks = partial_value.reshape(partial_value.shape[0], 2, tile_width, tile_width)
    mirrored = jnp.swapaxes(blocks[:, ::-1], 2, 3)
    return (blocks - mirrored).reshape(partial_value.shape)


def pair_energies(eps_occ, pair_list):
    occ_ids = lax.broadcasted_iota(jnp.int32, (1, 1, eps_occ.shape[0]), 2)
    one_hot = pair_list[:, :, None] == occ_ids
    return jnp.sum(jnp.where(one_hot, eps_occ[None, None, :], jnp.float32(0.0)), axis=(1, 2))


def sum_to_owners(antisym):
    return lax.psum_scatter(antisym, "virt", scatter_dimension=1, tiled=True)


def updated(ladder, eps_occ, eps_vir, pair_list):
    tile_width = eps_vir.shape[0] // 2
    column_count = ladder.shape[1]
    energy_tiles = eps_vir.reshape(2, tile_width)
    virt_energy = (energy_tiles[:, :, None] + energy_tiles[::-1][:, None, :]).reshape(
        2 * tile_width * tile_width
    )
    local_energy = lax.dynamic_slice_in_dim(
        virt_energy, lax.axis_index("virt") * column_count, column_count
    )
    pair_energy = pair_energies(eps_occ, pair_list)
    return ladder / (pair_energy[:, None] - local_energy[None, :])


def any_mesh_body(amplitudes, integrals, eps_occ, eps_vir, pair_list):
    tile_width = eps_vir.shape[0] // 2
    by_pairs = lax.dot_general(
        lax.all_gather(amplitudes, "pair", axis=0, tiled=True),
        integrals,
        (((1,), (1,)), ((), ())),
        precision=lax.Precision.HIGHEST,
        preferred_element_type=jnp.float32,
    )
    partial_value = lax.all_to_all(by_pairs, "pair", split_axis=0, concat_axis=1, tiled=True)
    ladder = sum_to_owners(antisymmetrize(partial_value, tile_width))
    return (ladder, updated(ladder, eps_occ, eps_vir, pair_list))


def split(value):
    high = value.astype(jnp.bfloat16)
    return high, (value - high.astype(jnp.float32)).astype(jnp.bfloat16)


def times(left, right):
    return lax.dot_general(
        left, right, (((1,), (1,)), ((), ())), preferred_element_type=jnp.float32
    )


def ladder_kernel(
    h, amp_ref, int_ref, out_ref, own, stage, int_high, int_low, blocks, weights, ct_ref,
    got, summed, rows, diff, below, above, sums, relayed, kept, other, placed,
    own_sem, stage_sem, amp_send, amp_recv,
    core_send, core_recv, pair_send, pair_recv,
    main_send, side_send, below_recv, above_recv, last_send, last_recv,
):
    r = lax.axis_index("pair")
    v = lax.axis_index("virt")
    z = v // 2
    c = v % 2
    mate = v + 1 - 2 * c
    x = r % 2
    y = r // 2
    peers = (y * 2 + (1 - x), (1 - y) * 2 + x, (1 - y) * 2 + (1 - x))
    count, depth = own.shape
    third = depth // 3
    sizes = (third, third // 2, third, third // 2)
    starts = (0, third, third + third // 2, 2 * third + third // 2)
    step = stage.shape[1]
    steps = int_ref.shape[0] // step

    own_copy = pltpu.make_async_copy(amp_ref, own, own_sem)
    own_copy.start()

    def stage_copy(t):
        return pltpu.make_async_copy(
            int_ref.at[pl.ds(pl.multiple_of(t * step, 8), step)],
            stage.at[t % 2],
            stage_sem.at[t % 2],
        )

    stage_copy(0).start()
    stage_copy(1).start()

    barrier = pltpu.get_barrier_semaphore()
    pl.semaphore_signal(barrier, inc=1, device_id={"virt": mate}, device_id_type=MESH)
    for peer in peers:
        pl.semaphore_signal(barrier, inc=1, device_id={"pair": peer}, device_id_type=MESH)

    @pl.when(z < 3)
    def _():
        pl.semaphore_signal(barrier, inc=1, device_id={"virt": v + 2}, device_id_type=MESH)

    @pl.when(z > 0)
    def _():
        pl.semaphore_signal(barrier, inc=1, device_id={"virt": v - 2}, device_id_type=MESH)

    across = (v + 4) % 8
    pl.semaphore_signal(barrier, inc=1, device_id={"virt": across}, device_id_type=MESH)
    inner = jnp.logical_and(z > 0, z < 3)

    @pl.when(inner)
    def _():
        pl.semaphore_wait(barrier, 7)

    @pl.when(jnp.logical_not(inner))
    def _():
        pl.semaphore_wait(barrier, 6)

    def columns_of(part):
        return pl.ds(starts[part], sizes[part])

    def amp_copy(d, part):
        return pltpu.make_async_remote_copy(
            src_ref=amp_ref.at[:, columns_of(part)],
            dst_ref=blocks.at[d, :, columns_of(part)],
            send_sem=amp_send,
            recv_sem=amp_recv.at[d, part],
            device_id={"pair": peers[d]},
            device_id_type=MESH,
        )

    def pass_on(part):
        d = part // 2
        return pltpu.make_async_remote_copy(
            src_ref=blocks.at[d, :, columns_of(part)],
            dst_ref=blocks.at[2, :, columns_of(part)],
            send_sem=amp_send,
            recv_sem=amp_recv.at[2, part],
            device_id={"pair": peers[1 - d]},
            device_id_type=MESH,
        )

    for parts in zip((0, 1, 2, 3), (2, 0, 1, 3)):
        for d in range(2):
            amp_copy(d, parts[d]).start()

    def weigh(source, high_at, low_at, start, size):
        wide = 2 * LANES

        @pl.loop(0, size // wide)
        def _(k):
            columns = pl.ds(pl.multiple_of(start + k * wide, wide), wide)
            value = source[:, columns]
            if count < LANES:
                value = jnp.concatenate(
                    [value, jnp.zeros((LANES - count, wide), jnp.float32)], axis=0
                )
            high, low = split(value)
            weights[pl.ds(high_at * LANES, LANES), columns] = high
            weights[pl.ds(low_at * LANES, LANES), columns] = low

    def keep(t, size, lanes, value, first):
        per = size // (4 * h)
        i = t // (h // per)
        at = pl.multiple_of(t % (h // per) * per, per)
        place = (i, pl.ds(at, per), slice(None), slice(None), slice(None), lanes)
        value = value.reshape(per, 2, 2, h, value.shape[1])
        ct_ref[place] = value if first else ct_ref[place] + value

    def one_block(high, low, at, columns):
        both = times(high, weights[pl.ds(at * LANES, 2 * LANES), columns])
        rest = times(low, weights[pl.ds(at * LANES, LANES), columns])
        return both[:, :LANES] + both[:, LANES:] + rest

    own_copy.wait()
    weigh(own, 0, 1, 0, depth)

    @pl.loop(0, steps)
    def _(t):
        stage_copy(t).wait()
        high, low = split(stage[t % 2])
        at = pl.ds(pl.multiple_of(t * step, 16), step)
        int_high[at, :] = high
        int_low[at, :] = low

        @pl.when(t + 2 < steps)
        def _():
            stage_copy(t + 2).start()

        value = one_block(int_high[at, :], int_low[at, :], 0, slice(None))
        keep(t, step, pl.ds(3 * LANES, LANES), value, True)

    order = (peers[2], peers[0], peers[1], r)

    def core_copy(n, i):
        return pltpu.make_async_remote_copy(
            src_ref=ct_ref.at[i, :, :, (1 - c + i) % 2, :, pl.ds(n * LANES, LANES)],
            dst_ref=got.at[n, i],
            send_sem=core_send,
            recv_sem=core_recv.at[n, i],
            device_id={"virt": mate},
            device_id_type=MESH,
        )

    def pair_copy(n, piece, i):
        bh = (x if n == 2 else 1 - x) if piece == 0 else (1 - x if n == 2 else x)
        return pltpu.make_async_remote_copy(
            src_ref=summed.at[n, pl.ds(i * h, h), bh],
            dst_ref=rows.at[r, pl.ds(i * h, h), bh],
            send_sem=pair_send,
            recv_sem=pair_recv.at[n, piece, i],
            device_id={"pair": order[n]},
            device_id_type=MESH,
        )

    def core_add(n, i):
        lanes = pl.ds(n * LANES, LANES)
        core_copy(n, i).wait_recv()

        @pl.loop(0, h, unroll=4)
        def _(a):
            for bh in range(2):
                total = ct_ref[i, a, bh, (c + i) % 2, :, lanes] + got[n, i, a, bh]
                if n < 3:
                    summed[n, i * h + a, bh] = total
                else:
                    rows[r, i * h + a, bh] = total

    big = 2 * step
    half = steps // 4

    def near_block(i, start, size, first):
        columns = pl.ds(start, size)

        @pl.loop(i * half, (i + 1) * half)
        def _(t):
            at = pl.ds(pl.multiple_of(t * big, 16), big)
            near_high = weights[pl.ds(4 * LANES, 2 * LANES), columns]
            near_low = weights[pl.ds(6 * LANES, 2 * LANES), columns]
            value = times(int_high[at, columns], near_high)
            value = value + times(int_high[at, columns], near_low)
            value = value + times(int_low[at, columns], near_high)
            keep(t, big, pl.ds(LANES, 2 * LANES), value, first)

    for i in range(2):
        core_copy(3, i).start()
    amp_copy(0, 0).wait_recv()
    pass_on(0).start()
    amp_copy(1, 2).wait_recv()
    pass_on(2).start()
    amp_copy(1, 0).wait_recv()
    for d in range(2):
        weigh(blocks.at[d], 4 + d, 6 + d, starts[0], sizes[0])
    for i in range(2):
        near_block(i, starts[0], sizes[0], True)
    amp_copy(0, 1).wait_recv()
    pass_on(1).start()
    for i in range(2):
        core_add(3, i)
    amp_copy(1, 1).wait_recv()
    amp_copy(0, 2).wait_recv()
    for d in range(2):
        weigh(blocks.at[d], 4 + d, 6 + d, starts[1], sizes[1] + sizes[2])
    for i in range(2):
        near_block(i, starts[1], sizes[1] + sizes[2], False)
    amp_copy(1, 3).wait_recv()
    pass_on(3).start()
    amp_copy(0, 3).wait_recv()
    for d in range(2):
        weigh(blocks.at[d], 4 + d, 6 + d, starts[3], sizes[3])
    for i in range(2):
        near_block(i, starts[3], sizes[3], False)
        core_copy(2, i).start()
        core_copy(1, i).start()
    for i in range(2):
        core_add(2, i)
        pair_copy(2, 0, i).start()
        core_add(1, i)
        pair_copy(1, 0, i).start()
    for n in (2, 1):
        for i in range(2):
            pair_copy(n, 1, i).start()

    def far_block(i, parts, first):
        @pl.loop(i * half, (i + 1) * half)
        def _(t):
            at = pl.ds(pl.multiple_of(t * big, 16), big)
            values = [
                one_block(int_high[at, columns_of(p)], int_low[at, columns_of(p)], 2, columns_of(p))
                for p in parts
            ]
            keep(t, big, pl.ds(0, LANES), values[0] + values[1], first)

    for parts in ((0, 2), (1, 3)):
        for p in parts:
            pass_on(p).wait_recv()
            weigh(blocks.at[2], 2, 3, starts[p], sizes[p])
        for i in range(2):
            far_block(i, parts, parts[0] == 0)
            if parts[0] == 1:
                core_copy(0, i).start()

    def antisym(q, i, u, size):
        ah = q // 2
        bh = q % 2
        mirror = (c + i) % 2
        rises = h // 4

        @pl.loop(0, size * rises, unroll=4)
        def _(n):
            a = u * rises + n
            plain = rows[ah, i * h + a, bh]
            turned = rows[2 + bh, pl.ds(mirror * h, h), ah, a, :]
            at = q * 8 + i * 4 + u + n // rises
            diff[at, pl.ds(pl.multiple_of(n % rises * h, 8), h), :] = plain - turned

    def main_copy(upwards, q, k, size, direct, step_at):
        far_up = jnp.where(z == 0, 0, q % 2) if direct else 0
        far_down = jnp.where(z == 3, 0, 1 - q // 2) if direct else 0
        at = pl.ds(k, size)
        return pltpu.make_async_remote_copy(
            src_ref=sums.at[at],
            dst_ref=(below if upwards else above).at[at],
            send_sem=main_send,
            recv_sem=(below_recv if upwards else above_recv).at[step_at],
            device_id={"virt": v + 2 + 2 * far_up if upwards else v - 2 - 2 * far_down},
            device_id_type=MESH,
        )

    def relay_copy(upwards, k, size, step_at):
        at = pl.ds(k, size)
        return pltpu.make_async_remote_copy(
            src_ref=relayed.at[at],
            dst_ref=(below if upwards else above).at[at],
            send_sem=side_send,
            recv_sem=(below_recv if upwards else above_recv).at[step_at],
            device_id={"virt": v + 2 if upwards else v - 2},
            device_id_type=MESH,
        )

    def side_copy(upwards, k, size, step_at):
        at = pl.ds(k, size)
        return pltpu.make_async_remote_copy(
            src_ref=diff.at[at],
            dst_ref=(above if upwards else below).at[at],
            send_sem=side_send,
            recv_sem=(above_recv if upwards else below_recv).at[step_at],
            device_id={"virt": v + 2 if upwards else v - 2},
            device_id_type=MESH,
        )

    def side_down(q):
        return jnp.logical_and(z == 1, q // 2 == 0)

    def side_up(q):
        return jnp.logical_and(z == 2, q % 2 == 1)

    def near(q, k, size, direct, step_at):
        at = pl.ds(k, size)
        if direct:

            @pl.when(side_down(q))
            def _():
                side_copy(False, k, size, step_at).start()

            @pl.when(side_up(q))
            def _():
                side_copy(True, k, size, step_at).start()

        @pl.when(jnp.logical_not(inner))
        def _():
            sums[at] = diff[at]

        @pl.when(z == 1)
        def _():
            main_copy(True, q, k, size, direct, step_at).wait_recv()
            sums[at] = diff[at] + below[at]

        @pl.when(z == 2)
        def _():
            main_copy(False, q, k, size, direct, step_at).wait_recv()
            sums[at] = diff[at] + above[at]

        @pl.when(z < 2)
        def _():
            main_copy(True, q, k, size, direct, step_at).start()

        @pl.when(z >= 2)
        def _():
            main_copy(False, q, k, size, direct, step_at).start()

    def relay(q, k, size, step_at):
        at = pl.ds(k, size)

        @pl.when(z == 1)
        def _():
            relay_copy(False, k, size, step_at).wait_recv()

        @pl.when(z == 2)
        def _():
            relay_copy(True, k, size, step_at).wait_recv()

        @pl.when(side_down(q))
        def _():
            relayed[at] = diff[at] + above[at]
            relay_copy(False, k, size, step_at).start()

        @pl.when(side_up(q))
        def _():
            relayed[at] = diff[at] + below[at]
            relay_copy(True, k, size, step_at).start()

    def last_copy(t, u, size):
        at = pl.ds(pl.multiple_of(u * piece_rows, 8), size * piece_rows)
        return pltpu.make_async_remote_copy(
            src_ref=other.at[t, at],
            dst_ref=kept.at[1, t, at],
            send_sem=last_send,
            recv_sem=last_recv.at[t, u],
            device_id={"virt": mate},
            device_id_type=MESH,
        )

    piece_rows = h * h // 4
    ours = jnp.where(z < 2, c, 0)

    def owned_here(q):
        return jnp.where(z < 2, q // 2 == z, q % 2 == z - 2)

    def place_of(q):
        return jnp.where(z < 2, q % 2, q // 2)

    def finish(q, i, u, size, direct, step_at):
        k = q * 8 + i * 4 + u
        at = pl.ds(k, size)
        t = place_of(q)
        to = pl.ds(pl.multiple_of(u * piece_rows, 8), size * piece_rows)

        @pl.when(owned_here(q))
        def _():
            @pl.when(z != 1 if direct else z == 3)
            def _():
                main_copy(True, q, k, size, direct, step_at).wait_recv()

            @pl.when(z != 2 if direct else z == 0)
            def _():
                main_copy(False, q, k, size, direct, step_at).wait_recv()

            low = below[at]
            high = above[at]
            if not direct:
                low = jnp.where(z > 0, low, jnp.float32(0.0))
                high = jnp.where(z < 3, high, jnp.float32(0.0))
            total = (diff[at] + low + high).reshape(size * piece_rows, LANES)

            @pl.when(i == ours)
            def _():
                kept[0, t, to] = total

            @pl.when(i != ours)
            def _():
                other[t, to] = total
                last_copy(t, u, size).start()

    alike = x * 3
    unlike = (1 - x) * 3
    mixed_near = jnp.where(y == 0, (1 - x) * 2 + x, x * 2 + 1 - x)
    mixed_far = jnp.where(y == 0, x * 2 + 1 - x, (1 - x) * 2 + x)
    quads = (alike, mixed_near, mixed_far, unlike)
    turns = [jnp.where(y == 0, (t + c) % 2, t) for t in range(2)]
    mate_turns = [jnp.where(y == 0, (t + 1 - c) % 2, t) for t in range(2)]
    mate_ours = jnp.where(z < 2, 1 - c, 0)
    needs = (
        ((2, 0, 0),), ((2, 0, 1),),
        ((1, 0, 0), (1, 0, 1), (2, 1, 0)), ((2, 1, 1),),
        ((0, 0, 0),), ((0, 0, 1),),
        ((1, 1, 0), (1, 1, 1), (0, 1, 0)), ((0, 1, 1),),
    )
    todo = []
    for g in range(4):
        for t in range(2):
            direct = g == 3 and t == 1
            size = 1 if direct else 2
            for u in range(0, 4, size):
                todo.append((g, t, u, size, direct))
    lag = 4
    later = 6
    for s, (g, t, u, size, direct) in enumerate(todo):
        q = quads[g]
        if u == 0:
            for n, piece, i in needs[g * 2 + t]:
                pair_copy(n, piece, i).wait_recv()
        antisym(q, turns[t], u, size)
        near(q, q * 8 + turns[t] * 4 + u, size, direct, s)
        if s == 1:
            for i in range(2):
                core_add(0, i)
            for piece in range(2):
                for i in range(2):
                    pair_copy(0, piece, i).start()
        if s >= lag:
            eg, et, eu, esize, edirect = todo[s - lag]
            if not edirect:

                @pl.when(inner)
                def _():
                    relay(quads[eg], quads[eg] * 8 + turns[et] * 4 + eu, esize, s - lag)

        if s >= later:
            eg, et, eu, esize, edirect = todo[s - later]

            @pl.when(inner)
            def _():
                finish(quads[eg], turns[et], eu, esize, edirect, s - later)

    @pl.when(jnp.logical_not(inner))
    def _():
        for s, (g, t, u, size, direct) in enumerate(todo[: len(todo) - later]):
            finish(quads[g], turns[t], u, size, direct, s)

    for s in range(len(todo) - later, len(todo)):
        g, t, u, size, direct = todo[s]
        finish(quads[g], turns[t], u, size, direct, s)

    def put(s, t):
        @pl.loop(0, h, unroll=4)
        def _(a):
            at = pl.multiple_of((a * 4 + 2 * t + s) * h, 8)
            plain = kept[s, t, pl.ds(pl.multiple_of(a * h, 8), h), :]
            turned = kept[s, t, pl.ds(a, h, stride=h), :]
            placed[pl.ds(at, h), :] = jnp.where(z < 2, plain, turned)

    for t in range(2):
        put(0, t)
    for g, t, u, size, direct in todo:
        q = quads[g]

        @pl.when(jnp.logical_and(owned_here(q), mate_turns[t] != mate_ours))
        def _():
            last_copy(place_of(q), u, size).wait_recv()

    for t in range(2):
        put(1, t)

    for n in range(out_ref.shape[1] // LANES):
        at = pl.ds(n * LANES, LANES)
        out_ref[:, at] = placed[at, :].T[:count]

    def wait_sent(buffer, sem):
        pltpu.make_async_remote_copy(
            src_ref=buffer, dst_ref=buffer, send_sem=sem, recv_sem=own_sem,
            device_id={"virt": mate}, device_id_type=MESH,
        ).wait_send()

    wait_sent(blocks, amp_send)
    wait_sent(got, core_send)
    wait_sent(summed, pair_send)
    wait_sent(sums, main_send)
    wait_sent(other, last_send)

    @pl.when(inner)
    def _():
        wait_sent(relayed.at[pl.ds(0, 16)], side_send)


def ladder_of(amplitudes, integrals, tile_width):
    h = tile_width // 4
    count, depth = amplitudes.shape
    owned = integrals.shape[0]
    step = owned // 8
    f32 = jnp.float32
    bf16 = jnp.bfloat16
    dma = pltpu.SemaphoreType.DMA
    return pl.pallas_call(
        functools.partial(ladder_kernel, h),
        out_shape=pltpu.VMEM((count, tile_width * h), f32),
        in_specs=[pl.BlockSpec(memory_space=pl.ANY), pl.BlockSpec(memory_space=pl.ANY)],
        out_specs=pl.BlockSpec(memory_space=pltpu.VMEM),
        scratch_shapes=[
            pltpu.VMEM((count, depth), f32),
            pltpu.VMEM((2, step, depth), f32),
            pltpu.VMEM((owned, depth), bf16),
            pltpu.VMEM((owned, depth), bf16),
            pltpu.VMEM((3, count, depth), f32),
            pltpu.VMEM((8 * LANES, depth), bf16),
            pltpu.VMEM((2, h, 2, 2, h, 4 * LANES), f32),
            pltpu.VMEM((4, 2, h, 2, h, LANES), f32),
            pltpu.VMEM((3, 2 * h, 2, h, LANES), f32),
            pltpu.VMEM((4, 2 * h, 2, h, LANES), f32),
            pltpu.VMEM((32, h * h // 4, LANES), f32),
            pltpu.VMEM((32, h * h // 4, LANES), f32),
            pltpu.VMEM((32, h * h // 4, LANES), f32),
            pltpu.VMEM((32, h * h // 4, LANES), f32),
            pltpu.VMEM((32, h * h // 4, LANES), f32),
            pltpu.VMEM((2, 2, h * h, LANES), f32),
            pltpu.VMEM((2, h * h, LANES), f32),
            pltpu.VMEM((tile_width * h, LANES), f32),
            dma, dma((2,)), dma, dma((3, 4)),
            dma, dma((4, 2)), dma, dma((3, 2, 2)),
            dma, dma, dma((18,)), dma((18,)), dma, dma((2, 4)),
        ],
        compiler_params=pltpu.CompilerParams(
            collective_id=0, has_side_effects=True, vmem_limit_bytes=58 * 1024 * 1024
        ),
        name="ladder",
    )(amplitudes, integrals)


def block_body(amplitudes, integrals, eps_occ, eps_vir, pair_list):
    tile_width = eps_vir.shape[0] // 2
    first = lax.axis_index("virt") < lax.axis_size("virt") // 2
    sign = jnp.where(first, jnp.float32(1.0), jnp.float32(-1.0))
    raw = ladder_of(amplitudes, integrals, tile_width)
    raw, eps_occ, eps_vir, pair_list = lax.optimization_barrier(
        (raw, eps_occ, eps_vir, pair_list)
    )
    ladder = sign * raw
    return (ladder, updated(ladder, eps_occ, eps_vir, pair_list))


def solution(mesh):
    in_specs = (P("pair", "virt"), P("pair", "virt"), P(), P(), P("pair", None))
    out_specs = (P("pair", "virt"), P("pair", "virt"))
    fits = mesh.shape["pair"] == 4 and mesh.shape["virt"] == 8

    def body(amplitudes, integrals, eps_occ, eps_vir, pair_list):
        tiled = eps_vir.shape[0] % 64 == 0 and amplitudes.shape[0] <= LANES
        tiled = tiled and amplitudes.shape[1] % (12 * LANES) == 0
        chosen = block_body if fits and tiled else any_mesh_body
        return chosen(amplitudes, integrals, eps_occ, eps_vir, pair_list)

    return jax.shard_map(body, mesh=mesh, in_specs=in_specs, out_specs=out_specs, check_vma=False)
```

```python
import functools

import jax
import jax.numpy as jnp
from jax import lax
from jax.experimental import pallas as pl
from jax.experimental.pallas import tpu as pltpu
from jax.sharding import PartitionSpec as P

MESH = pl.DeviceIdType.MESH
LANES = 128


def antisymmetrize(partial_value, tile_width):
    blocks = partial_value.reshape(partial_value.shape[0], 2, tile_width, tile_width)
    mirrored = jnp.swapaxes(blocks[:, ::-1], 2, 3)
    return (blocks - mirrored).reshape(partial_value.shape)


def pair_energies(eps_occ, pair_list):
    occ_ids = lax.broadcasted_iota(jnp.int32, (1, 1, eps_occ.shape[0]), 2)
    one_hot = pair_list[:, :, None] == occ_ids
    return jnp.sum(jnp.where(one_hot, eps_occ[None, None, :], jnp.float32(0.0)), axis=(1, 2))


def sum_to_owners(antisym):
    return lax.psum_scatter(antisym, "virt", scatter_dimension=1, tiled=True)


def updated(ladder, eps_occ, eps_vir, pair_list):
    tile_width = eps_vir.shape[0] // 2
    column_count = ladder.shape[1]
    energy_tiles = eps_vir.reshape(2, tile_width)
    virt_energy = (energy_tiles[:, :, None] + energy_tiles[::-1][:, None, :]).reshape(
        2 * tile_width * tile_width
    )
    local_energy = lax.dynamic_slice_in_dim(
        virt_energy, lax.axis_index("virt") * column_count, column_count
    )
    pair_energy = pair_energies(eps_occ, pair_list)
    return ladder / (pair_energy[:, None] - local_energy[None, :])


def any_mesh_body(amplitudes, integrals, eps_occ, eps_vir, pair_list):
    tile_width = eps_vir.shape[0] // 2
    by_pairs = lax.dot_general(
        lax.all_gather(amplitudes, "pair", axis=0, tiled=True),
        integrals,
        (((1,), (1,)), ((), ())),
        precision=lax.Precision.HIGHEST,
        preferred_element_type=jnp.float32,
    )
    partial_value = lax.all_to_all(by_pairs, "pair", split_axis=0, concat_axis=1, tiled=True)
    ladder = sum_to_owners(antisymmetrize(partial_value, tile_width))
    return (ladder, updated(ladder, eps_occ, eps_vir, pair_list))


def split(value):
    high = value.astype(jnp.bfloat16)
    return high, (value - high.astype(jnp.float32)).astype(jnp.bfloat16)


def times(left, right):
    return lax.dot_general(
        left, right, (((1,), (1,)), ((), ())), preferred_element_type=jnp.float32
    )


def ladder_kernel(
    h, amp_ref, int_ref, out_ref, own, stage, int_high, int_low, blocks, weights, ct_ref,
    got, summed, rows, diff, below, above, sums, relayed, kept, other, placed,
    own_sem, stage_sem, amp_send, amp_recv,
    core_send, core_recv, pair_send, pair_recv,
    main_send, side_send, below_recv, above_recv, last_send, last_recv,
):
    r = lax.axis_index("pair")
    v = lax.axis_index("virt")
    z = v // 2
    c = v % 2
    mate = v + 1 - 2 * c
    x = r % 2
    y = r // 2
    peers = (y * 2 + (1 - x), (1 - y) * 2 + x, (1 - y) * 2 + (1 - x))
    count, depth = own.shape
    third = depth // 3
    sizes = (third, third // 2, third, third // 2)
    starts = (0, third, third + third // 2, 2 * third + third // 2)
    step = stage.shape[1]
    steps = int_ref.shape[0] // step

    own_copy = pltpu.make_async_copy(amp_ref, own, own_sem)
    own_copy.start()

    def stage_copy(t):
        return pltpu.make_async_copy(
            int_ref.at[pl.ds(pl.multiple_of(t * step, 8), step)],
            stage.at[t % 2],
            stage_sem.at[t % 2],
        )

    stage_copy(0).start()
    stage_copy(1).start()

    barrier = pltpu.get_barrier_semaphore()
    pl.semaphore_signal(barrier, inc=1, device_id={"virt": mate}, device_id_type=MESH)
    for peer in peers:
        pl.semaphore_signal(barrier, inc=1, device_id={"pair": peer}, device_id_type=MESH)

    @pl.when(z < 3)
    def _():
        pl.semaphore_signal(barrier, inc=1, device_id={"virt": v + 2}, device_id_type=MESH)

    @pl.when(z > 0)
    def _():
        pl.semaphore_signal(barrier, inc=1, device_id={"virt": v - 2}, device_id_type=MESH)

    inner = jnp.logical_and(z > 0, z < 3)

    @pl.when(inner)
    def _():
        pl.semaphore_wait(barrier, 6)

    @pl.when(jnp.logical_not(inner))
    def _():
        pl.semaphore_wait(barrier, 5)

    def columns_of(part):
        return pl.ds(starts[part], sizes[part])

    def amp_copy(d, part):
        return pltpu.make_async_remote_copy(
            src_ref=amp_ref.at[:, columns_of(part)],
            dst_ref=blocks.at[d, :, columns_of(part)],
            send_sem=amp_send,
            recv_sem=amp_recv.at[d, part],
            device_id={"pair": peers[d]},
            device_id_type=MESH,
        )

    def pass_on(part):
        d = part // 2
        return pltpu.make_async_remote_copy(
            src_ref=blocks.at[d, :, columns_of(part)],
            dst_ref=blocks.at[2, :, columns_of(part)],
            send_sem=amp_send,
            recv_sem=amp_recv.at[2, part],
            device_id={"pair": peers[1 - d]},
            device_id_type=MESH,
        )

    for parts in zip((0, 1, 2, 3), (2, 0, 1, 3)):
        for d in range(2):
            amp_copy(d, parts[d]).start()

    def weigh(source, high_at, low_at, start, size):
        wide = 2 * LANES

        @pl.loop(0, size // wide)
        def _(k):
            columns = pl.ds(pl.multiple_of(start + k * wide, wide), wide)
            value = source[:, columns]
            if count < LANES:
                value = jnp.concatenate(
                    [value, jnp.zeros((LANES - count, wide), jnp.float32)], axis=0
                )
            high, low = split(value)
            weights[pl.ds(high_at * LANES, LANES), columns] = high
            weights[pl.ds(low_at * LANES, LANES), columns] = low

    def keep(t, size, lanes, value, first):
        per = size // (4 * h)
        i = t // (h // per)
        at = pl.multiple_of(t % (h // per) * per, per)
        place = (i, pl.ds(at, per), slice(None), slice(None), slice(None), lanes)
        value = value.reshape(per, 2, 2, h, value.shape[1])
        ct_ref[place] = value if first else ct_ref[place] + value

    def one_block(high, low, at, columns):
        both = times(high, weights[pl.ds(at * LANES, 2 * LANES), columns])
        rest = times(low, weights[pl.ds(at * LANES, LANES), columns])
        return both[:, :LANES] + both[:, LANES:] + rest

    own_copy.wait()
    weigh(own, 0, 1, 0, depth)

    @pl.loop(0, steps)
    def _(t):
        stage_copy(t).wait()
        high, low = split(stage[t % 2])
        at = pl.ds(pl.multiple_of(t * step, 16), step)
        int_high[at, :] = high
        int_low[at, :] = low

        @pl.when(t + 2 < steps)
        def _():
            stage_copy(t + 2).start()

        value = one_block(int_high[at, :], int_low[at, :], 0, slice(None))
        keep(t, step, pl.ds(3 * LANES, LANES), value, True)

    order = (peers[2], peers[0], peers[1], r)

    def core_copy(n, i):
        return pltpu.make_async_remote_copy(
            src_ref=ct_ref.at[i, :, :, (1 - c + i) % 2, :, pl.ds(n * LANES, LANES)],
            dst_ref=got.at[n, i],
            send_sem=core_send,
            recv_sem=core_recv.at[n, i],
            device_id={"virt": mate},
            device_id_type=MESH,
        )

    def pair_copy(n, piece, i):
        bh = (x if n == 2 else 1 - x) if piece == 0 else (1 - x if n == 2 else x)
        return pltpu.make_async_remote_copy(
            src_ref=summed.at[n, pl.ds(i * h, h), bh],
            dst_ref=rows.at[r, pl.ds(i * h, h), bh],
            send_sem=pair_send,
            recv_sem=pair_recv.at[n, piece, i],
            device_id={"pair": order[n]},
            device_id_type=MESH,
        )

    def core_add(n, i):
        lanes = pl.ds(n * LANES, LANES)
        core_copy(n, i).wait_recv()

        @pl.loop(0, h, unroll=4)
        def _(a):
            for bh in range(2):
                total = ct_ref[i, a, bh, (c + i) % 2, :, lanes] + got[n, i, a, bh]
                if n < 3:
                    summed[n, i * h + a, bh] = total
                else:
                    rows[r, i * h + a, bh] = total

    big = 2 * step
    half = steps // 4

    def near_block(i, start, size, first):
        columns = pl.ds(start, size)

        @pl.loop(i * half, (i + 1) * half)
        def _(t):
            at = pl.ds(pl.multiple_of(t * big, 16), big)
            near_high = weights[pl.ds(4 * LANES, 2 * LANES), columns]
            near_low = weights[pl.ds(6 * LANES, 2 * LANES), columns]
            value = times(int_high[at, columns], near_high)
            value = value + times(int_high[at, columns], near_low)
            value = value + times(int_low[at, columns], near_high)
            keep(t, big, pl.ds(LANES, 2 * LANES), value, first)

    for i in range(2):
        core_copy(3, i).start()
    amp_copy(0, 0).wait_recv()
    pass_on(0).start()
    amp_copy(1, 2).wait_recv()
    pass_on(2).start()
    amp_copy(1, 0).wait_recv()
    for d in range(2):
        weigh(blocks.at[d], 4 + d, 6 + d, starts[0], sizes[0])
    for i in range(2):
        near_block(i, starts[0], sizes[0], True)
    amp_copy(0, 1).wait_recv()
    pass_on(1).start()
    for i in range(2):
        core_add(3, i)
    amp_copy(1, 1).wait_recv()
    amp_copy(0, 2).wait_recv()
    for d in range(2):
        weigh(blocks.at[d], 4 + d, 6 + d, starts[1], sizes[1] + sizes[2])
    for i in range(2):
        near_block(i, starts[1], sizes[1] + sizes[2], False)
    amp_copy(1, 3).wait_recv()
    pass_on(3).start()
    amp_copy(0, 3).wait_recv()
    for d in range(2):
        weigh(blocks.at[d], 4 + d, 6 + d, starts[3], sizes[3])
    for i in range(2):
        near_block(i, starts[3], sizes[3], False)
        core_copy(2, i).start()
        core_copy(1, i).start()
    for i in range(2):
        core_add(2, i)
        pair_copy(2, 0, i).start()
        core_add(1, i)
        pair_copy(1, 0, i).start()
    for n in (2, 1):
        for i in range(2):
            pair_copy(n, 1, i).start()

    def far_block(i, parts, first):
        @pl.loop(i * half, (i + 1) * half)
        def _(t):
            at = pl.ds(pl.multiple_of(t * big, 16), big)
            values = [
                one_block(int_high[at, columns_of(p)], int_low[at, columns_of(p)], 2, columns_of(p))
                for p in parts
            ]
            keep(t, big, pl.ds(0, LANES), values[0] + values[1], first)

    for parts in ((0, 2), (1, 3)):
        for p in parts:
            pass_on(p).wait_recv()
            weigh(blocks.at[2], 2, 3, starts[p], sizes[p])
        for i in range(2):
            far_block(i, parts, parts[0] == 0)
            if parts[0] == 1:
                core_copy(0, i).start()

    def antisym(q, i, u, size):
        ah = q // 2
        bh = q % 2
        mirror = (c + i) % 2
        rises = h // 4

        @pl.loop(0, size * rises, unroll=4)
        def _(n):
            a = u * rises + n
            plain = rows[ah, i * h + a, bh]
            turned = rows[2 + bh, pl.ds(mirror * h, h), ah, a, :]
            at = q * 8 + i * 4 + u + n // rises
            diff[at, pl.ds(pl.multiple_of(n % rises * h, 8), h), :] = plain - turned

    def main_copy(upwards, q, k, size, step_at):
        at = pl.ds(k, size)
        return pltpu.make_async_remote_copy(
            src_ref=sums.at[at],
            dst_ref=(below if upwards else above).at[at],
            send_sem=main_send,
            recv_sem=(below_recv if upwards else above_recv).at[step_at],
            device_id={"virt": v + 2 if upwards else v - 2},
            device_id_type=MESH,
        )

    def relay_copy(upwards, k, size, step_at):
        at = pl.ds(k, size)
        return pltpu.make_async_remote_copy(
            src_ref=relayed.at[at],
            dst_ref=(below if upwards else above).at[at],
            send_sem=side_send,
            recv_sem=(below_recv if upwards else above_recv).at[step_at],
            device_id={"virt": v + 2 if upwards else v - 2},
            device_id_type=MESH,
        )

    def sends_down(q):
        return jnp.logical_and(z == 1, q // 2 == 0)

    def sends_up(q):
        return jnp.logical_and(z == 2, q % 2 == 1)

    def near(q, k, size, step_at):
        at = pl.ds(k, size)
        @pl.when(jnp.logical_not(inner))
        def _():
            sums[at] = diff[at]

        @pl.when(z == 1)
        def _():
            main_copy(True, q, k, size, step_at).wait_recv()
            sums[at] = diff[at] + below[at]

        @pl.when(z == 2)
        def _():
            main_copy(False, q, k, size, step_at).wait_recv()
            sums[at] = diff[at] + above[at]

        @pl.when(z < 2)
        def _():
            main_copy(True, q, k, size, step_at).start()

        @pl.when(z >= 2)
        def _():
            main_copy(False, q, k, size, step_at).start()

    def relay(q, k, size, step_at):
        at = pl.ds(k, size)

        @pl.when(z == 1)
        def _():
            relay_copy(False, k, size, step_at).wait_recv()

        @pl.when(z == 2)
        def _():
            relay_copy(True, k, size, step_at).wait_recv()

        @pl.when(sends_down(q))
        def _():
            relayed[at] = diff[at] + above[at]
            relay_copy(False, k, size, step_at).start()

        @pl.when(sends_up(q))
        def _():
            relayed[at] = diff[at] + below[at]
            relay_copy(True, k, size, step_at).start()

    def last_copy(t, u, size):
        at = pl.ds(pl.multiple_of(u * piece_rows, 8), size * piece_rows)
        return pltpu.make_async_remote_copy(
            src_ref=other.at[t, at],
            dst_ref=kept.at[1, t, at],
            send_sem=last_send,
            recv_sem=last_recv.at[t, u],
            device_id={"virt": mate},
            device_id_type=MESH,
        )

    piece_rows = h * h // 4
    ours = jnp.where(z < 2, c, 0)

    def owned_here(q):
        return jnp.where(z < 2, q // 2 == z, q % 2 == z - 2)

    def place_of(q):
        return jnp.where(z < 2, q % 2, q // 2)

    def finish(q, i, u, size, step_at):
        k = q * 8 + i * 4 + u
        at = pl.ds(k, size)
        t = place_of(q)
        to = pl.ds(pl.multiple_of(u * piece_rows, 8), size * piece_rows)

        @pl.when(owned_here(q))
        def _():
            @pl.when(z == 3)
            def _():
                main_copy(True, q, k, size, step_at).wait_recv()

            @pl.when(z == 0)
            def _():
                main_copy(False, q, k, size, step_at).wait_recv()

            low = jnp.where(z > 0, below[at], jnp.float32(0.0))
            high = jnp.where(z < 3, above[at], jnp.float32(0.0))
            total = (diff[at] + low + high).reshape(size * piece_rows, LANES)

            @pl.when(i == ours)
            def _():
                kept[0, t, to] = total

            @pl.when(i != ours)
            def _():
                other[t, to] = total
                last_copy(t, u, size).start()

    alike = x * 3
    unlike = (1 - x) * 3
    mixed_near = jnp.where(y == 0, (1 - x) * 2 + x, x * 2 + 1 - x)
    mixed_far = jnp.where(y == 0, x * 2 + 1 - x, (1 - x) * 2 + x)
    quads = (alike, mixed_near, mixed_far, unlike)
    turns = [jnp.where(y == 0, (t + c) % 2, t) for t in range(2)]
    mate_turns = [jnp.where(y == 0, (t + 1 - c) % 2, t) for t in range(2)]
    mate_ours = jnp.where(z < 2, 1 - c, 0)
    needs = (
        ((2, 0, 0),), ((2, 0, 1),),
        ((1, 0, 0), (1, 0, 1), (2, 1, 0)), ((2, 1, 1),),
        ((0, 0, 0),), ((0, 0, 1),),
        ((1, 1, 0), (1, 1, 1), (0, 1, 0)), ((0, 1, 1),),
    )
    todo = []
    for g in range(4):
        for t in range(2):
            size = 1 if g == 3 and t == 1 else 2
            for u in range(0, 4, size):
                todo.append((g, t, u, size))
    lag = 3
    later = 6
    for s, (g, t, u, size) in enumerate(todo):
        q = quads[g]
        if u == 0:
            for n, piece, i in needs[g * 2 + t]:
                pair_copy(n, piece, i).wait_recv()
        antisym(q, turns[t], u, size)
        near(q, q * 8 + turns[t] * 4 + u, size, s)
        if s == 1:
            for i in range(2):
                core_add(0, i)
            for piece in range(2):
                for i in range(2):
                    pair_copy(0, piece, i).start()
        if s >= lag:
            eg, et, eu, esize = todo[s - lag]

            @pl.when(inner)
            def _():
                relay(quads[eg], quads[eg] * 8 + turns[et] * 4 + eu, esize, s - lag)

        if s >= later:
            eg, et, eu, esize = todo[s - later]

            @pl.when(inner)
            def _():
                finish(quads[eg], turns[et], eu, esize, s - later)

    @pl.when(jnp.logical_not(inner))
    def _():
        for s, (g, t, u, size) in enumerate(todo[: len(todo) - later]):
            finish(quads[g], turns[t], u, size, s)

    for s in range(len(todo) - later, len(todo)):
        g, t, u, size = todo[s]
        if s >= len(todo) - lag:

            @pl.when(inner)
            def _():
                relay(quads[g], quads[g] * 8 + turns[t] * 4 + u, size, s)

        finish(quads[g], turns[t], u, size, s)

    def put(s, t):
        @pl.loop(0, h, unroll=4)
        def _(a):
            at = pl.multiple_of((a * 4 + 2 * t + s) * h, 8)
            plain = kept[s, t, pl.ds(pl.multiple_of(a * h, 8), h), :]
            turned = kept[s, t, pl.ds(a, h, stride=h), :]
            placed[pl.ds(at, h), :] = jnp.where(z < 2, plain, turned)

    for t in range(2):
        put(0, t)
    for g, t, u, size in todo:
        q = quads[g]

        @pl.when(jnp.logical_and(owned_here(q), mate_turns[t] != mate_ours))
        def _():
            last_copy(place_of(q), u, size).wait_recv()

    for t in range(2):
        put(1, t)

    for n in range(out_ref.shape[1] // LANES):
        at = pl.ds(n * LANES, LANES)
        out_ref[:, at] = placed[at, :].T[:count]

    def wait_sent(buffer, sem):
        pltpu.make_async_remote_copy(
            src_ref=buffer, dst_ref=buffer, send_sem=sem, recv_sem=own_sem,
            device_id={"virt": mate}, device_id_type=MESH,
        ).wait_send()

    wait_sent(blocks, amp_send)
    wait_sent(got, core_send)
    wait_sent(summed, pair_send)
    wait_sent(sums, main_send)
    wait_sent(other, last_send)

    @pl.when(inner)
    def _():
        wait_sent(relayed.at[pl.ds(0, 16)], side_send)


def ladder_of(amplitudes, integrals, tile_width):
    h = tile_width // 4
    count, depth = amplitudes.shape
    owned = integrals.shape[0]
    step = owned // 8
    f32 = jnp.float32
    bf16 = jnp.bfloat16
    dma = pltpu.SemaphoreType.DMA
    return pl.pallas_call(
        functools.partial(ladder_kernel, h),
        out_shape=pltpu.VMEM((count, tile_width * h), f32),
        in_specs=[pl.BlockSpec(memory_space=pl.ANY), pl.BlockSpec(memory_space=pl.ANY)],
        out_specs=pl.BlockSpec(memory_space=pltpu.VMEM),
        scratch_shapes=[
            pltpu.VMEM((count, depth), f32),
            pltpu.VMEM((2, step, depth), f32),
            pltpu.VMEM((owned, depth), bf16),
            pltpu.VMEM((owned, depth), bf16),
            pltpu.VMEM((3, count, depth), f32),
            pltpu.VMEM((8 * LANES, depth), bf16),
            pltpu.VMEM((2, h, 2, 2, h, 4 * LANES), f32),
            pltpu.VMEM((4, 2, h, 2, h, LANES), f32),
            pltpu.VMEM((3, 2 * h, 2, h, LANES), f32),
            pltpu.VMEM((4, 2 * h, 2, h, LANES), f32),
            pltpu.VMEM((32, h * h // 4, LANES), f32),
            pltpu.VMEM((32, h * h // 4, LANES), f32),
            pltpu.VMEM((32, h * h // 4, LANES), f32),
            pltpu.VMEM((32, h * h // 4, LANES), f32),
            pltpu.VMEM((32, h * h // 4, LANES), f32),
            pltpu.VMEM((2, 2, h * h, LANES), f32),
            pltpu.VMEM((2, h * h, LANES), f32),
            pltpu.VMEM((tile_width * h, LANES), f32),
            dma, dma((2,)), dma, dma((3, 4)),
            dma, dma((4, 2)), dma, dma((3, 2, 2)),
            dma, dma, dma((18,)), dma((18,)), dma, dma((2, 4)),
        ],
        compiler_params=pltpu.CompilerParams(
            collective_id=0, has_side_effects=True, vmem_limit_bytes=58 * 1024 * 1024
        ),
        name="ladder",
    )(amplitudes, integrals)


def block_body(amplitudes, integrals, eps_occ, eps_vir, pair_list):
    tile_width = eps_vir.shape[0] // 2
    first = lax.axis_index("virt") < lax.axis_size("virt") // 2
    sign = jnp.where(first, jnp.float32(1.0), jnp.float32(-1.0))
    raw = ladder_of(amplitudes, integrals, tile_width)
    raw, eps_occ, eps_vir, pair_list = lax.optimization_barrier(
        (raw, eps_occ, eps_vir, pair_list)
    )
    ladder = sign * raw
    return (ladder, updated(ladder, eps_occ, eps_vir, pair_list))


def solution(mesh):
    in_specs = (P("pair", "virt"), P("pair", "virt"), P(), P(), P("pair", None))
    out_specs = (P("pair", "virt"), P("pair", "virt"))
    fits = mesh.shape["pair"] == 4 and mesh.shape["virt"] == 8

    def body(amplitudes, integrals, eps_occ, eps_vir, pair_list):
        tiled = eps_vir.shape[0] % 64 == 0 and amplitudes.shape[0] <= LANES
        tiled = tiled and amplitudes.shape[1] % (12 * LANES) == 0
        chosen = block_body if fits and tiled else any_mesh_body
        return chosen(amplitudes, integrals, eps_occ, eps_vir, pair_list)

    return jax.shard_map(body, mesh=mesh, in_specs=in_specs, out_specs=out_specs, check_vma=False)
```

```python
import functools

import jax
import jax.numpy as jnp
from jax import lax
from jax.experimental import pallas as pl
from jax.experimental.pallas import tpu as pltpu
from jax.sharding import PartitionSpec as P

MESH = pl.DeviceIdType.MESH
LANES = 128


def antisymmetrize(partial_value, tile_width):
    blocks = partial_value.reshape(partial_value.shape[0], 2, tile_width, tile_width)
    mirrored = jnp.swapaxes(blocks[:, ::-1], 2, 3)
    return (blocks - mirrored).reshape(partial_value.shape)


def pair_energies(eps_occ, pair_list):
    occ_ids = lax.broadcasted_iota(jnp.int32, (1, 1, eps_occ.shape[0]), 2)
    one_hot = pair_list[:, :, None] == occ_ids
    return jnp.sum(jnp.where(one_hot, eps_occ[None, None, :], jnp.float32(0.0)), axis=(1, 2))


def sum_to_owners(antisym):
    return lax.psum_scatter(antisym, "virt", scatter_dimension=1, tiled=True)


def updated(ladder, eps_occ, eps_vir, pair_list):
    tile_width = eps_vir.shape[0] // 2
    column_count = ladder.shape[1]
    energy_tiles = eps_vir.reshape(2, tile_width)
    virt_energy = (energy_tiles[:, :, None] + energy_tiles[::-1][:, None, :]).reshape(
        2 * tile_width * tile_width
    )
    local_energy = lax.dynamic_slice_in_dim(
        virt_energy, lax.axis_index("virt") * column_count, column_count
    )
    pair_energy = pair_energies(eps_occ, pair_list)
    return ladder / (pair_energy[:, None] - local_energy[None, :])


def any_mesh_body(amplitudes, integrals, eps_occ, eps_vir, pair_list):
    tile_width = eps_vir.shape[0] // 2
    by_pairs = lax.dot_general(
        lax.all_gather(amplitudes, "pair", axis=0, tiled=True),
        integrals,
        (((1,), (1,)), ((), ())),
        precision=lax.Precision.HIGHEST,
        preferred_element_type=jnp.float32,
    )
    partial_value = lax.all_to_all(by_pairs, "pair", split_axis=0, concat_axis=1, tiled=True)
    ladder = sum_to_owners(antisymmetrize(partial_value, tile_width))
    return (ladder, updated(ladder, eps_occ, eps_vir, pair_list))


def split(value):
    high = value.astype(jnp.bfloat16)
    return high, (value - high.astype(jnp.float32)).astype(jnp.bfloat16)


def times(left, right):
    return lax.dot_general(
        left, right, (((1,), (1,)), ((), ())), preferred_element_type=jnp.float32
    )


def ladder_kernel(
    h, amp_ref, int_ref, out_ref, own, stage, int_high, int_low, blocks, weights, ct_ref,
    got, summed, rows, diff, below, above, sums, relayed, kept, other, placed,
    own_sem, stage_sem, amp_send, amp_recv,
    core_send, core_recv, pair_send, pair_recv,
    main_send, side_send, below_recv, above_recv, last_send, last_recv,
):
    r = lax.axis_index("pair")
    v = lax.axis_index("virt")
    z = v // 2
    c = v % 2
    mate = v + 1 - 2 * c
    x = r % 2
    y = r // 2
    peers = (y * 2 + (1 - x), (1 - y) * 2 + x, (1 - y) * 2 + (1 - x))
    count, depth = own.shape
    third = depth // 3
    sizes = (third, third // 2, third, third // 2)
    starts = (0, third, third + third // 2, 2 * third + third // 2)
    step = stage.shape[1]
    steps = int_ref.shape[0] // step

    own_copy = pltpu.make_async_copy(amp_ref, own, own_sem)
    own_copy.start()

    def stage_copy(t):
        return pltpu.make_async_copy(
            int_ref.at[pl.ds(pl.multiple_of(t * step, 8), step)],
            stage.at[t % 2],
            stage_sem.at[t % 2],
        )

    stage_copy(0).start()
    stage_copy(1).start()

    barrier = pltpu.get_barrier_semaphore()
    pl.semaphore_signal(barrier, inc=1, device_id={"virt": mate}, device_id_type=MESH)
    for peer in peers:
        pl.semaphore_signal(barrier, inc=1, device_id={"pair": peer}, device_id_type=MESH)

    @pl.when(z < 3)
    def _():
        pl.semaphore_signal(barrier, inc=1, device_id={"virt": v + 2}, device_id_type=MESH)

    @pl.when(z > 0)
    def _():
        pl.semaphore_signal(barrier, inc=1, device_id={"virt": v - 2}, device_id_type=MESH)

    inner = jnp.logical_and(z > 0, z < 3)

    @pl.when(inner)
    def _():
        pl.semaphore_wait(barrier, 6)

    @pl.when(jnp.logical_not(inner))
    def _():
        pl.semaphore_wait(barrier, 5)

    def columns_of(part):
        return pl.ds(starts[part], sizes[part])

    def amp_copy(d, part):
        return pltpu.make_async_remote_copy(
            src_ref=amp_ref.at[:, columns_of(part)],
            dst_ref=blocks.at[d, :, columns_of(part)],
            send_sem=amp_send,
            recv_sem=amp_recv.at[d, part],
            device_id={"pair": peers[d]},
            device_id_type=MESH,
        )

    def pass_on(part):
        d = part // 2
        return pltpu.make_async_remote_copy(
            src_ref=blocks.at[d, :, columns_of(part)],
            dst_ref=blocks.at[2, :, columns_of(part)],
            send_sem=amp_send,
            recv_sem=amp_recv.at[2, part],
            device_id={"pair": peers[1 - d]},
            device_id_type=MESH,
        )

    for parts in zip((0, 1, 2, 3), (2, 0, 1, 3)):
        for d in range(2):
            amp_copy(d, parts[d]).start()

    def weigh(source, high_at, low_at, start, size):
        wide = 2 * LANES

        @pl.loop(0, size // wide)
        def _(k):
            columns = pl.ds(pl.multiple_of(start + k * wide, wide), wide)
            value = source[:, columns]
            if count < LANES:
                value = jnp.concatenate(
                    [value, jnp.zeros((LANES - count, wide), jnp.float32)], axis=0
                )
            high, low = split(value)
            weights[pl.ds(high_at * LANES, LANES), columns] = high
            weights[pl.ds(low_at * LANES, LANES), columns] = low

    def keep(t, size, lanes, value, first):
        per = size // (4 * h)
        i = t // (h // per)
        at = pl.multiple_of(t % (h // per) * per, per)
        place = (i, pl.ds(at, per), slice(None), slice(None), slice(None), lanes)
        value = value.reshape(per, 2, 2, h, value.shape[1])
        ct_ref[place] = value if first else ct_ref[place] + value

    def one_block(high, low, at, columns):
        both = times(high, weights[pl.ds(at * LANES, 2 * LANES), columns])
        rest = times(low, weights[pl.ds(at * LANES, LANES), columns])
        return both[:, :LANES] + both[:, LANES:] + rest

    own_copy.wait()
    weigh(own, 0, 1, 0, depth)

    @pl.loop(0, steps)
    def _(t):
        stage_copy(t).wait()
        high, low = split(stage[t % 2])
        at = pl.ds(pl.multiple_of(t * step, 16), step)
        int_high[at, :] = high
        int_low[at, :] = low

        @pl.when(t + 2 < steps)
        def _():
            stage_copy(t + 2).start()

        value = one_block(int_high[at, :], int_low[at, :], 0, slice(None))
        keep(t, step, pl.ds(3 * LANES, LANES), value, True)

    order = (peers[2], peers[0], peers[1], r)

    def core_copy(n, i):
        return pltpu.make_async_remote_copy(
            src_ref=ct_ref.at[i, :, :, (1 - c + i) % 2, :, pl.ds(n * LANES, LANES)],
            dst_ref=got.at[n, i],
            send_sem=core_send,
            recv_sem=core_recv.at[n, i],
            device_id={"virt": mate},
            device_id_type=MESH,
        )

    def pair_copy(n, piece, i):
        bh = (x if n == 2 else 1 - x) if piece == 0 else (1 - x if n == 2 else x)
        return pltpu.make_async_remote_copy(
            src_ref=summed.at[n, pl.ds(i * h, h), bh],
            dst_ref=rows.at[r, pl.ds(i * h, h), bh],
            send_sem=pair_send,
            recv_sem=pair_recv.at[n, piece, i],
            device_id={"pair": order[n]},
            device_id_type=MESH,
        )

    def core_add(n, i):
        lanes = pl.ds(n * LANES, LANES)
        core_copy(n, i).wait_recv()

        @pl.loop(0, h, unroll=4)
        def _(a):
            for bh in range(2):
                total = ct_ref[i, a, bh, (c + i) % 2, :, lanes] + got[n, i, a, bh]
                if n < 3:
                    summed[n, i * h + a, bh] = total
                else:
                    rows[r, i * h + a, bh] = total

    big = 2 * step
    half = steps // 4

    def near_block(i, start, size, first):
        columns = pl.ds(start, size)

        @pl.loop(i * half, (i + 1) * half)
        def _(t):
            at = pl.ds(pl.multiple_of(t * big, 16), big)
            near_high = weights[pl.ds(4 * LANES, 2 * LANES), columns]
            near_low = weights[pl.ds(6 * LANES, 2 * LANES), columns]
            value = times(int_high[at, columns], near_high)
            value = value + times(int_high[at, columns], near_low)
            value = value + times(int_low[at, columns], near_high)
            keep(t, big, pl.ds(LANES, 2 * LANES), value, first)

    for i in range(2):
        core_copy(3, i).start()
    amp_copy(0, 0).wait_recv()
    pass_on(0).start()
    amp_copy(1, 2).wait_recv()
    pass_on(2).start()
    amp_copy(1, 0).wait_recv()
    for d in range(2):
        weigh(blocks.at[d], 4 + d, 6 + d, starts[0], sizes[0])
    for i in range(2):
        near_block(i, starts[0], sizes[0], True)
    amp_copy(0, 1).wait_recv()
    pass_on(1).start()
    for i in range(2):
        core_add(3, i)
    amp_copy(1, 1).wait_recv()
    amp_copy(0, 2).wait_recv()
    for d in range(2):
        weigh(blocks.at[d], 4 + d, 6 + d, starts[1], sizes[1] + sizes[2])
    for i in range(2):
        near_block(i, starts[1], sizes[1] + sizes[2], False)
    amp_copy(1, 3).wait_recv()
    pass_on(3).start()
    amp_copy(0, 3).wait_recv()
    for d in range(2):
        weigh(blocks.at[d], 4 + d, 6 + d, starts[3], sizes[3])
    for i in range(2):
        near_block(i, starts[3], sizes[3], False)
        core_copy(2, i).start()
        core_copy(1, i).start()
    for i in range(2):
        core_add(2, i)
        pair_copy(2, 0, i).start()
        core_add(1, i)
        pair_copy(1, 0, i).start()
    for n in (2, 1):
        for i in range(2):
            pair_copy(n, 1, i).start()

    def far_block(i, parts, first):
        @pl.loop(i * half, (i + 1) * half)
        def _(t):
            at = pl.ds(pl.multiple_of(t * big, 16), big)
            values = [
                one_block(int_high[at, columns_of(p)], int_low[at, columns_of(p)], 2, columns_of(p))
                for p in parts
            ]
            keep(t, big, pl.ds(0, LANES), values[0] + values[1], first)

    for parts in ((0, 2), (1, 3)):
        for p in parts:
            pass_on(p).wait_recv()
            weigh(blocks.at[2], 2, 3, starts[p], sizes[p])
        for i in range(2):
            far_block(i, parts, parts[0] == 0)
            if parts[0] == 1:
                core_copy(0, i).start()

    def antisym(q, i, u, size):
        ah = q // 2
        bh = q % 2
        mirror = (c + i) % 2
        rises = h // 4

        @pl.loop(0, size * rises, unroll=4)
        def _(n):
            a = u * rises + n
            plain = rows[ah, i * h + a, bh]
            turned = rows[2 + bh, pl.ds(mirror * h, h), ah, a, :]
            at = q * 8 + i * 4 + u + n // rises
            diff[at, pl.ds(pl.multiple_of(n % rises * h, 8), h), :] = plain - turned

    def main_copy(upwards, q, k, size, step_at):
        at = pl.ds(k, size)
        return pltpu.make_async_remote_copy(
            src_ref=sums.at[at],
            dst_ref=(below if upwards else above).at[at],
            send_sem=main_send,
            recv_sem=(below_recv if upwards else above_recv).at[step_at],
            device_id={"virt": v + 2 if upwards else v - 2},
            device_id_type=MESH,
        )

    def relay_copy(upwards, k, size, step_at):
        at = pl.ds(k, size)
        return pltpu.make_async_remote_copy(
            src_ref=relayed.at[at],
            dst_ref=(below if upwards else above).at[at],
            send_sem=side_send,
            recv_sem=(below_recv if upwards else above_recv).at[step_at],
            device_id={"virt": v + 2 if upwards else v - 2},
            device_id_type=MESH,
        )

    def sends_down(q):
        return jnp.logical_and(z == 1, q // 2 == 0)

    def sends_up(q):
        return jnp.logical_and(z == 2, q % 2 == 1)

    def near(q, k, size, step_at):
        at = pl.ds(k, size)
        @pl.when(jnp.logical_not(inner))
        def _():
            sums[at] = diff[at]

        @pl.when(z == 1)
        def _():
            main_copy(True, q, k, size, step_at).wait_recv()
            sums[at] = diff[at] + below[at]

        @pl.when(z == 2)
        def _():
            main_copy(False, q, k, size, step_at).wait_recv()
            sums[at] = diff[at] + above[at]

        @pl.when(z < 2)
        def _():
            main_copy(True, q, k, size, step_at).start()

        @pl.when(z >= 2)
        def _():
            main_copy(False, q, k, size, step_at).start()

    def relay(q, k, size, step_at):
        at = pl.ds(k, size)

        @pl.when(z == 1)
        def _():
            relay_copy(False, k, size, step_at).wait_recv()

        @pl.when(z == 2)
        def _():
            relay_copy(True, k, size, step_at).wait_recv()

        @pl.when(sends_down(q))
        def _():
            relayed[at] = diff[at] + above[at]
            relay_copy(False, k, size, step_at).start()

        @pl.when(sends_up(q))
        def _():
            relayed[at] = diff[at] + below[at]
            relay_copy(True, k, size, step_at).start()

    def last_copy(t, u, size):
        at = pl.ds(pl.multiple_of(u * piece_rows, 8), size * piece_rows)
        return pltpu.make_async_remote_copy(
            src_ref=other.at[t, at],
            dst_ref=kept.at[1, t, at],
            send_sem=last_send,
            recv_sem=last_recv.at[t, u],
            device_id={"virt": mate},
            device_id_type=MESH,
        )

    piece_rows = h * h // 4
    ours = jnp.where(z < 2, c, 0)

    def owned_here(q):
        return jnp.where(z < 2, q // 2 == z, q % 2 == z - 2)

    def place_of(q):
        return jnp.where(z < 2, q % 2, q // 2)

    def finish(q, i, u, size, step_at):
        k = q * 8 + i * 4 + u
        at = pl.ds(k, size)
        t = place_of(q)
        to = pl.ds(pl.multiple_of(u * piece_rows, 8), size * piece_rows)

        @pl.when(owned_here(q))
        def _():
            @pl.when(z == 3)
            def _():
                main_copy(True, q, k, size, step_at).wait_recv()

            @pl.when(z == 0)
            def _():
                main_copy(False, q, k, size, step_at).wait_recv()

            low = jnp.where(z > 0, below[at], jnp.float32(0.0))
            high = jnp.where(z < 3, above[at], jnp.float32(0.0))
            total = (diff[at] + low + high).reshape(size * piece_rows, LANES)

            @pl.when(i == ours)
            def _():
                kept[0, t, to] = total

            @pl.when(i != ours)
            def _():
                other[t, to] = total
                last_copy(t, u, size).start()

    alike = x * 3
    unlike = (1 - x) * 3
    mixed_near = jnp.where(y == 0, (1 - x) * 2 + x, x * 2 + 1 - x)
    mixed_far = jnp.where(y == 0, x * 2 + 1 - x, (1 - x) * 2 + x)
    quads = (alike, mixed_near, mixed_far, unlike)
    turns = [jnp.where(y == 0, (t + c) % 2, t) for t in range(2)]
    mate_turns = [jnp.where(y == 0, (t + 1 - c) % 2, t) for t in range(2)]
    mate_ours = jnp.where(z < 2, 1 - c, 0)
    needs = (
        ((2, 0, 0),), ((2, 0, 1),),
        ((1, 0, 0), (1, 0, 1), (2, 1, 0)), ((2, 1, 1),),
        ((0, 0, 0),), ((0, 0, 1),),
        ((1, 1, 0), (1, 1, 1), (0, 1, 0)), ((0, 1, 1),),
    )
    todo = []
    for g in range(4):
        for t in range(2):
            size = 2
            for u in range(0, 4, size):
                todo.append((g, t, u, size))
    lag = 3
    later = 6
    for s, (g, t, u, size) in enumerate(todo):
        q = quads[g]
        if u == 0:
            for n, piece, i in needs[g * 2 + t]:
                pair_copy(n, piece, i).wait_recv()
        antisym(q, turns[t], u, size)
        near(q, q * 8 + turns[t] * 4 + u, size, s)
        if s == 1:
            for i in range(2):
                core_add(0, i)
            for piece in range(2):
                for i in range(2):
                    pair_copy(0, piece, i).start()
        if s >= lag:
            eg, et, eu, esize = todo[s - lag]

            @pl.when(inner)
            def _():
                relay(quads[eg], quads[eg] * 8 + turns[et] * 4 + eu, esize, s - lag)

        if s >= later:
            eg, et, eu, esize = todo[s - later]

            @pl.when(inner)
            def _():
                finish(quads[eg], turns[et], eu, esize, s - later)

    @pl.when(jnp.logical_not(inner))
    def _():
        for s, (g, t, u, size) in enumerate(todo[: len(todo) - later]):
            finish(quads[g], turns[t], u, size, s)

    for s in range(len(todo) - later, len(todo)):
        g, t, u, size = todo[s]
        if s >= len(todo) - lag:

            @pl.when(inner)
            def _():
                relay(quads[g], quads[g] * 8 + turns[t] * 4 + u, size, s)

        finish(quads[g], turns[t], u, size, s)

    def put(s, t):
        @pl.loop(0, h, unroll=4)
        def _(a):
            at = pl.multiple_of((a * 4 + 2 * t + s) * h, 8)
            plain = kept[s, t, pl.ds(pl.multiple_of(a * h, 8), h), :]
            turned = kept[s, t, pl.ds(a, h, stride=h), :]
            placed[pl.ds(at, h), :] = jnp.where(z < 2, plain, turned)

    for t in range(2):
        put(0, t)
    for g, t, u, size in todo:
        q = quads[g]

        @pl.when(jnp.logical_and(owned_here(q), mate_turns[t] != mate_ours))
        def _():
            last_copy(place_of(q), u, size).wait_recv()

    for t in range(2):
        put(1, t)

    for n in range(out_ref.shape[1] // LANES):
        at = pl.ds(n * LANES, LANES)
        out_ref[:, at] = placed[at, :].T[:count]

    def wait_sent(buffer, sem):
        pltpu.make_async_remote_copy(
            src_ref=buffer, dst_ref=buffer, send_sem=sem, recv_sem=own_sem,
            device_id={"virt": mate}, device_id_type=MESH,
        ).wait_send()

    wait_sent(blocks, amp_send)
    wait_sent(got, core_send)
    wait_sent(summed, pair_send)
    wait_sent(sums, main_send)
    wait_sent(other, last_send)

    @pl.when(inner)
    def _():
        wait_sent(relayed.at[pl.ds(0, 16)], side_send)


def ladder_of(amplitudes, integrals, tile_width):
    h = tile_width // 4
    count, depth = amplitudes.shape
    owned = integrals.shape[0]
    step = owned // 8
    f32 = jnp.float32
    bf16 = jnp.bfloat16
    dma = pltpu.SemaphoreType.DMA
    return pl.pallas_call(
        functools.partial(ladder_kernel, h),
        out_shape=pltpu.VMEM((count, tile_width * h), f32),
        in_specs=[pl.BlockSpec(memory_space=pl.ANY), pl.BlockSpec(memory_space=pl.ANY)],
        out_specs=pl.BlockSpec(memory_space=pltpu.VMEM),
        scratch_shapes=[
            pltpu.VMEM((count, depth), f32),
            pltpu.VMEM((2, step, depth), f32),
            pltpu.VMEM((owned, depth), bf16),
            pltpu.VMEM((owned, depth), bf16),
            pltpu.VMEM((3, count, depth), f32),
            pltpu.VMEM((8 * LANES, depth), bf16),
            pltpu.VMEM((2, h, 2, 2, h, 4 * LANES), f32),
            pltpu.VMEM((4, 2, h, 2, h, LANES), f32),
            pltpu.VMEM((3, 2 * h, 2, h, LANES), f32),
            pltpu.VMEM((4, 2 * h, 2, h, LANES), f32),
            pltpu.VMEM((32, h * h // 4, LANES), f32),
            pltpu.VMEM((32, h * h // 4, LANES), f32),
            pltpu.VMEM((32, h * h // 4, LANES), f32),
            pltpu.VMEM((32, h * h // 4, LANES), f32),
            pltpu.VMEM((32, h * h // 4, LANES), f32),
            pltpu.VMEM((2, 2, h * h, LANES), f32),
            pltpu.VMEM((2, h * h, LANES), f32),
            pltpu.VMEM((tile_width * h, LANES), f32),
            dma, dma((2,)), dma, dma((3, 4)),
            dma, dma((4, 2)), dma, dma((3, 2, 2)),
            dma, dma, dma((16,)), dma((16,)), dma, dma((2, 4)),
        ],
        compiler_params=pltpu.CompilerParams(
            collective_id=0, has_side_effects=True, vmem_limit_bytes=58 * 1024 * 1024
        ),
        name="ladder",
    )(amplitudes, integrals)


def block_body(amplitudes, integrals, eps_occ, eps_vir, pair_list):
    tile_width = eps_vir.shape[0] // 2
    first = lax.axis_index("virt") < lax.axis_size("virt") // 2
    sign = jnp.where(first, jnp.float32(1.0), jnp.float32(-1.0))
    raw = ladder_of(amplitudes, integrals, tile_width)
    raw, eps_occ, eps_vir, pair_list = lax.optimization_barrier(
        (raw, eps_occ, eps_vir, pair_list)
    )
    ladder = sign * raw
    return (ladder, updated(ladder, eps_occ, eps_vir, pair_list))


def solution(mesh):
    in_specs = (P("pair", "virt"), P("pair", "virt"), P(), P(), P("pair", None))
    out_specs = (P("pair", "virt"), P("pair", "virt"))
    fits = mesh.shape["pair"] == 4 and mesh.shape["virt"] == 8

    def body(amplitudes, integrals, eps_occ, eps_vir, pair_list):
        tiled = eps_vir.shape[0] % 64 == 0 and amplitudes.shape[0] <= LANES
        tiled = tiled and amplitudes.shape[1] % (12 * LANES) == 0
        chosen = block_body if fits and tiled else any_mesh_body
        return chosen(amplitudes, integrals, eps_occ, eps_vir, pair_list)

    return jax.shard_map(body, mesh=mesh, in_specs=in_specs, out_specs=out_specs, check_vma=False)
```

```python
import functools

import jax
import jax.numpy as jnp
from jax import lax
from jax.experimental import pallas as pl
from jax.experimental.pallas import tpu as pltpu
from jax.sharding import PartitionSpec as P

MESH = pl.DeviceIdType.MESH
LANES = 128


def antisymmetrize(partial_value, tile_width):
    blocks = partial_value.reshape(partial_value.shape[0], 2, tile_width, tile_width)
    mirrored = jnp.swapaxes(blocks[:, ::-1], 2, 3)
    return (blocks - mirrored).reshape(partial_value.shape)


def pair_energies(eps_occ, pair_list):
    occ_ids = lax.broadcasted_iota(jnp.int32, (1, 1, eps_occ.shape[0]), 2)
    one_hot = pair_list[:, :, None] == occ_ids
    return jnp.sum(jnp.where(one_hot, eps_occ[None, None, :], jnp.float32(0.0)), axis=(1, 2))


def sum_to_owners(antisym):
    return lax.psum_scatter(antisym, "virt", scatter_dimension=1, tiled=True)


def updated(ladder, eps_occ, eps_vir, pair_list):
    tile_width = eps_vir.shape[0] // 2
    column_count = ladder.shape[1]
    energy_tiles = eps_vir.reshape(2, tile_width)
    virt_energy = (energy_tiles[:, :, None] + energy_tiles[::-1][:, None, :]).reshape(
        2 * tile_width * tile_width
    )
    local_energy = lax.dynamic_slice_in_dim(
        virt_energy, lax.axis_index("virt") * column_count, column_count
    )
    pair_energy = pair_energies(eps_occ, pair_list)
    return ladder / (pair_energy[:, None] - local_energy[None, :])


def any_mesh_body(amplitudes, integrals, eps_occ, eps_vir, pair_list):
    tile_width = eps_vir.shape[0] // 2
    by_pairs = lax.dot_general(
        lax.all_gather(amplitudes, "pair", axis=0, tiled=True),
        integrals,
        (((1,), (1,)), ((), ())),
        precision=lax.Precision.HIGHEST,
        preferred_element_type=jnp.float32,
    )
    partial_value = lax.all_to_all(by_pairs, "pair", split_axis=0, concat_axis=1, tiled=True)
    ladder = sum_to_owners(antisymmetrize(partial_value, tile_width))
    return (ladder, updated(ladder, eps_occ, eps_vir, pair_list))


def split(value):
    high = value.astype(jnp.bfloat16)
    return high, (value - high.astype(jnp.float32)).astype(jnp.bfloat16)


def times(left, right):
    return lax.dot_general(
        left, right, (((1,), (1,)), ((), ())), preferred_element_type=jnp.float32
    )


def ladder_kernel(
    h, amp_ref, int_ref, out_ref, own, stage, int_high, int_low, blocks, weights, ct_ref,
    got, summed, rows, diff, below, above, sums, relayed, kept, other, placed,
    own_sem, stage_sem, amp_send, amp_recv,
    core_send, core_recv, pair_send, pair_recv,
    main_send, side_send, below_recv, above_recv, last_send, last_recv,
):
    r = lax.axis_index("pair")
    v = lax.axis_index("virt")
    z = v // 2
    c = v % 2
    mate = v + 1 - 2 * c
    x = r % 2
    y = r // 2
    peers = (y * 2 + (1 - x), (1 - y) * 2 + x, (1 - y) * 2 + (1 - x))
    count, depth = own.shape
    third = depth // 3
    sizes = (third, third // 2, third, third // 2)
    starts = (0, third, third + third // 2, 2 * third + third // 2)
    step = stage.shape[1]
    steps = int_ref.shape[0] // step

    own_copy = pltpu.make_async_copy(amp_ref, own, own_sem)
    own_copy.start()

    def stage_copy(t):
        return pltpu.make_async_copy(
            int_ref.at[pl.ds(pl.multiple_of(t * step, 8), step)],
            stage.at[t % 2],
            stage_sem.at[t % 2],
        )

    stage_copy(0).start()
    stage_copy(1).start()

    barrier = pltpu.get_barrier_semaphore()
    pl.semaphore_signal(barrier, inc=1, device_id={"virt": mate}, device_id_type=MESH)
    for peer in peers:
        pl.semaphore_signal(barrier, inc=1, device_id={"pair": peer}, device_id_type=MESH)

    @pl.when(z < 3)
    def _():
        pl.semaphore_signal(barrier, inc=1, device_id={"virt": v + 2}, device_id_type=MESH)

    @pl.when(z > 0)
    def _():
        pl.semaphore_signal(barrier, inc=1, device_id={"virt": v - 2}, device_id_type=MESH)

    inner = jnp.logical_and(z > 0, z < 3)

    @pl.when(inner)
    def _():
        pl.semaphore_wait(barrier, 6)

    @pl.when(jnp.logical_not(inner))
    def _():
        pl.semaphore_wait(barrier, 5)

    def columns_of(part):
        return pl.ds(starts[part], sizes[part])

    def amp_copy(d, part):
        return pltpu.make_async_remote_copy(
            src_ref=amp_ref.at[:, columns_of(part)],
            dst_ref=blocks.at[d, :, columns_of(part)],
            send_sem=amp_send,
            recv_sem=amp_recv.at[d, part],
            device_id={"pair": peers[d]},
            device_id_type=MESH,
        )

    def pass_on(part):
        d = part // 2
        return pltpu.make_async_remote_copy(
            src_ref=blocks.at[d, :, columns_of(part)],
            dst_ref=blocks.at[2, :, columns_of(part)],
            send_sem=amp_send,
            recv_sem=amp_recv.at[2, part],
            device_id={"pair": peers[1 - d]},
            device_id_type=MESH,
        )

    for parts in zip((0, 1, 2, 3), (2, 0, 1, 3)):
        for d in range(2):
            amp_copy(d, parts[d]).start()

    def weigh(source, high_at, low_at, start, size):
        wide = 2 * LANES

        @pl.loop(0, size // wide)
        def _(k):
            columns = pl.ds(pl.multiple_of(start + k * wide, wide), wide)
            value = source[:, columns]
            if count < LANES:
                value = jnp.concatenate(
                    [value, jnp.zeros((LANES - count, wide), jnp.float32)], axis=0
                )
            high, low = split(value)
            weights[pl.ds(high_at * LANES, LANES), columns] = high
            weights[pl.ds(low_at * LANES, LANES), columns] = low

    def keep(t, size, lanes, value, first):
        per = size // (4 * h)
        i = t // (h // per)
        at = pl.multiple_of(t % (h // per) * per, per)
        place = (i, pl.ds(at, per), slice(None), slice(None), slice(None), lanes)
        value = value.reshape(per, 2, 2, h, value.shape[1])
        ct_ref[place] = value if first else ct_ref[place] + value

    def one_block(high, low, at, columns):
        both = times(high, weights[pl.ds(at * LANES, 2 * LANES), columns])
        rest = times(low, weights[pl.ds(at * LANES, LANES), columns])
        return both[:, :LANES] + both[:, LANES:] + rest

    own_copy.wait()
    weigh(own, 0, 1, 0, depth)

    @pl.loop(0, steps)
    def _(t):
        stage_copy(t).wait()
        high, low = split(stage[t % 2])
        at = pl.ds(pl.multiple_of(t * step, 16), step)
        int_high[at, :] = high
        int_low[at, :] = low

        @pl.when(t + 2 < steps)
        def _():
            stage_copy(t + 2).start()

        value = one_block(int_high[at, :], int_low[at, :], 0, slice(None))
        keep(t, step, pl.ds(3 * LANES, LANES), value, True)

    order = (peers[2], peers[0], peers[1], r)

    def core_copy(n, i):
        return pltpu.make_async_remote_copy(
            src_ref=ct_ref.at[i, :, :, (1 - c + i) % 2, :, pl.ds(n * LANES, LANES)],
            dst_ref=got.at[n, i],
            send_sem=core_send,
            recv_sem=core_recv.at[n, i],
            device_id={"virt": mate},
            device_id_type=MESH,
        )

    def pair_copy(n, piece, i):
        bh = (x if n == 2 else 1 - x) if piece == 0 else (1 - x if n == 2 else x)
        return pltpu.make_async_remote_copy(
            src_ref=summed.at[n, pl.ds(i * h, h), bh],
            dst_ref=rows.at[r, pl.ds(i * h, h), bh],
            send_sem=pair_send,
            recv_sem=pair_recv.at[n, piece, i],
            device_id={"pair": order[n]},
            device_id_type=MESH,
        )

    def core_add(n, i):
        lanes = pl.ds(n * LANES, LANES)
        core_copy(n, i).wait_recv()

        @pl.loop(0, h, unroll=4)
        def _(a):
            for bh in range(2):
                total = ct_ref[i, a, bh, (c + i) % 2, :, lanes] + got[n, i, a, bh]
                if n < 3:
                    summed[n, i * h + a, bh] = total
                else:
                    rows[r, i * h + a, bh] = total

    big = 2 * step
    half = steps // 4

    def near_block(i, start, size, first):
        columns = pl.ds(start, size)

        @pl.loop(i * half, (i + 1) * half)
        def _(t):
            at = pl.ds(pl.multiple_of(t * big, 16), big)
            near_high = weights[pl.ds(4 * LANES, 2 * LANES), columns]
            near_low = weights[pl.ds(6 * LANES, 2 * LANES), columns]
            value = times(int_high[at, columns], near_high)
            value = value + times(int_high[at, columns], near_low)
            value = value + times(int_low[at, columns], near_high)
            keep(t, big, pl.ds(LANES, 2 * LANES), value, first)

    for i in range(2):
        core_copy(3, i).start()
    amp_copy(0, 0).wait_recv()
    pass_on(0).start()
    amp_copy(1, 2).wait_recv()
    pass_on(2).start()
    amp_copy(1, 0).wait_recv()
    for d in range(2):
        weigh(blocks.at[d], 4 + d, 6 + d, starts[0], sizes[0])
    for i in range(2):
        near_block(i, starts[0], sizes[0], True)
    amp_copy(0, 1).wait_recv()
    pass_on(1).start()
    for i in range(2):
        core_add(3, i)
    amp_copy(1, 1).wait_recv()
    amp_copy(0, 2).wait_recv()
    for d in range(2):
        weigh(blocks.at[d], 4 + d, 6 + d, starts[1], sizes[1] + sizes[2])
    for i in range(2):
        near_block(i, starts[1], sizes[1] + sizes[2], False)
    amp_copy(1, 3).wait_recv()
    pass_on(3).start()
    amp_copy(0, 3).wait_recv()
    for d in range(2):
        weigh(blocks.at[d], 4 + d, 6 + d, starts[3], sizes[3])
    for i in range(2):
        near_block(i, starts[3], sizes[3], False)
        core_copy(2, i).start()
        core_copy(1, i).start()
    for i in range(2):
        core_add(2, i)
        pair_copy(2, 0, i).start()
        core_add(1, i)
        pair_copy(1, 0, i).start()
    for n in (2, 1):
        for i in range(2):
            pair_copy(n, 1, i).start()

    def far_block(i, parts, first):
        @pl.loop(i * half, (i + 1) * half)
        def _(t):
            at = pl.ds(pl.multiple_of(t * big, 16), big)
            values = [
                one_block(int_high[at, columns_of(p)], int_low[at, columns_of(p)], 2, columns_of(p))
                for p in parts
            ]
            keep(t, big, pl.ds(0, LANES), values[0] + values[1], first)

    for parts in ((0, 2), (1, 3)):
        for p in parts:
            pass_on(p).wait_recv()
            weigh(blocks.at[2], 2, 3, starts[p], sizes[p])
        for i in range(2):
            far_block(i, parts, parts[0] == 0)
            if parts[0] == 1:
                core_copy(0, i).start()

    def antisym(q, i, u, size):
        ah = q // 2
        bh = q % 2
        mirror = (c + i) % 2
        rises = h // 4

        @pl.loop(0, size * rises, unroll=4)
        def _(n):
            a = u * rises + n
            plain = rows[ah, i * h + a, bh]
            turned = rows[2 + bh, pl.ds(mirror * h, h), ah, a, :]
            at = q * 8 + i * 4 + u + n // rises
            diff[at, pl.ds(pl.multiple_of(n % rises * h, 8), h), :] = plain - turned

    def main_copy(upwards, q, k, size, step_at, source=None):
        at = pl.ds(k, size)
        return pltpu.make_async_remote_copy(
            src_ref=(sums if source is None else source).at[at],
            dst_ref=(below if upwards else above).at[at],
            send_sem=main_send,
            recv_sem=(below_recv if upwards else above_recv).at[step_at],
            device_id={"virt": v + 2 if upwards else v - 2},
            device_id_type=MESH,
        )

    def relay_copy(upwards, k, size, step_at):
        at = pl.ds(k, size)
        return pltpu.make_async_remote_copy(
            src_ref=relayed.at[at],
            dst_ref=(below if upwards else above).at[at],
            send_sem=side_send,
            recv_sem=(below_recv if upwards else above_recv).at[step_at],
            device_id={"virt": v + 2 if upwards else v - 2},
            device_id_type=MESH,
        )

    def sends_down(q):
        return jnp.logical_and(z == 1, q // 2 == 0)

    def sends_up(q):
        return jnp.logical_and(z == 2, q % 2 == 1)

    def near(q, k, size, step_at):
        at = pl.ds(k, size)
        @pl.when(z == 0)
        def _():
            main_copy(True, q, k, size, step_at, diff).start()

        @pl.when(z == 1)
        def _():
            main_copy(True, q, k, size, step_at).wait_recv()
            sums[at] = diff[at] + below[at]
            main_copy(True, q, k, size, step_at).start()

        @pl.when(z == 2)
        def _():
            main_copy(False, q, k, size, step_at).wait_recv()
            sums[at] = diff[at] + above[at]
            main_copy(False, q, k, size, step_at).start()

        @pl.when(z == 3)
        def _():
            main_copy(False, q, k, size, step_at, diff).start()

    def relay(q, k, size, step_at):
        at = pl.ds(k, size)

        @pl.when(z == 1)
        def _():
            relay_copy(False, k, size, step_at).wait_recv()

        @pl.when(z == 2)
        def _():
            relay_copy(True, k, size, step_at).wait_recv()

        @pl.when(sends_down(q))
        def _():
            relayed[at] = diff[at] + above[at]
            relay_copy(False, k, size, step_at).start()

        @pl.when(sends_up(q))
        def _():
            relayed[at] = diff[at] + below[at]
            relay_copy(True, k, size, step_at).start()

    def last_copy(t, u, size):
        at = pl.ds(pl.multiple_of(u * piece_rows, 8), size * piece_rows)
        return pltpu.make_async_remote_copy(
            src_ref=other.at[t, at],
            dst_ref=kept.at[1, t, at],
            send_sem=last_send,
            recv_sem=last_recv,
            device_id={"virt": mate},
            device_id_type=MESH,
        )

    piece_rows = h * h // 4
    ours = jnp.where(z < 2, c, 0)

    def owned_here(q):
        return jnp.where(z < 2, q // 2 == z, q % 2 == z - 2)

    def place_of(q):
        return jnp.where(z < 2, q % 2, q // 2)

    def finish(q, i, u, size, step_at):
        k = q * 8 + i * 4 + u
        at = pl.ds(k, size)
        t = place_of(q)
        to = pl.ds(pl.multiple_of(u * piece_rows, 8), size * piece_rows)

        @pl.when(owned_here(q))
        def _():
            @pl.when(z == 3)
            def _():
                main_copy(True, q, k, size, step_at).wait_recv()

            @pl.when(z == 0)
            def _():
                main_copy(False, q, k, size, step_at).wait_recv()

            low = jnp.where(z > 0, below[at], jnp.float32(0.0))
            high = jnp.where(z < 3, above[at], jnp.float32(0.0))
            total = (diff[at] + low + high).reshape(size * piece_rows, LANES)

            @pl.when(i == ours)
            def _():
                kept[0, t, to] = total

            @pl.when(i != ours)
            def _():
                other[t, to] = total
                last_copy(t, u, size).start()

    alike = x * 3
    unlike = (1 - x) * 3
    mixed_near = jnp.where(y == 0, (1 - x) * 2 + x, x * 2 + 1 - x)
    mixed_far = jnp.where(y == 0, x * 2 + 1 - x, (1 - x) * 2 + x)
    quads = (alike, mixed_near, mixed_far, unlike)
    turns = [jnp.where(y == 0, (t + c) % 2, t) for t in range(2)]
    needs = (
        ((2, 0, 0),), ((2, 0, 1),),
        ((1, 0, 0), (1, 0, 1), (2, 1, 0)), ((2, 1, 1),),
        ((0, 0, 0),), ((0, 0, 1),),
        ((1, 1, 0), (1, 1, 1), (0, 1, 0)), ((0, 1, 1),),
    )
    todo = []
    for g in range(4):
        for t in range(2):
            size = 1 if g == 3 and t == 1 else 2
            for u in range(0, 4, size):
                todo.append((g, t, u, size))
    lag = 3
    later = 6
    for s, (g, t, u, size) in enumerate(todo):
        q = quads[g]
        if u == 0:
            for n, piece, i in needs[g * 2 + t]:
                pair_copy(n, piece, i).wait_recv()
        antisym(q, turns[t], u, size)
        near(q, q * 8 + turns[t] * 4 + u, size, s)
        if s == 1:
            for i in range(2):
                core_add(0, i)
            for piece in range(2):
                for i in range(2):
                    pair_copy(0, piece, i).start()
        if s >= lag:
            eg, et, eu, esize = todo[s - lag]

            @pl.when(inner)
            def _():
                relay(quads[eg], quads[eg] * 8 + turns[et] * 4 + eu, esize, s - lag)

        if s >= later:
            eg, et, eu, esize = todo[s - later]

            @pl.when(inner)
            def _():
                finish(quads[eg], turns[et], eu, esize, s - later)

    @pl.when(jnp.logical_not(inner))
    def _():
        for s, (g, t, u, size) in enumerate(todo[: len(todo) - later]):
            finish(quads[g], turns[t], u, size, s)

    for s in range(len(todo) - later, len(todo)):
        g, t, u, size = todo[s]
        if s >= len(todo) - lag:

            @pl.when(inner)
            def _():
                relay(quads[g], quads[g] * 8 + turns[t] * 4 + u, size, s)

        finish(quads[g], turns[t], u, size, s)

    def put(s, t):
        @pl.loop(0, h, unroll=4)
        def _(a):
            at = pl.multiple_of((a * 4 + 2 * t + s) * h, 8)
            plain = kept[s, t, pl.ds(pl.multiple_of(a * h, 8), h), :]
            turned = kept[s, t, pl.ds(a, h, stride=h), :]
            placed[pl.ds(at, h), :] = jnp.where(z < 2, plain, turned)

    for t in range(2):
        put(0, t)
    pltpu.make_async_remote_copy(
        src_ref=other, dst_ref=kept.at[1], send_sem=last_send, recv_sem=last_recv,
        device_id={"virt": mate}, device_id_type=MESH,
    ).wait_recv()
    for t in range(2):
        put(1, t)

    for n in range(out_ref.shape[1] // LANES):
        at = pl.ds(n * LANES, LANES)
        out_ref[:, at] = placed[at, :].T[:count]

    def wait_sent(buffer, sem):
        pltpu.make_async_remote_copy(
            src_ref=buffer, dst_ref=buffer, send_sem=sem, recv_sem=own_sem,
            device_id={"virt": mate}, device_id_type=MESH,
        ).wait_send()

    wait_sent(blocks, amp_send)
    wait_sent(got, core_send)
    wait_sent(summed, pair_send)
    wait_sent(sums, main_send)
    wait_sent(other, last_send)

    @pl.when(inner)
    def _():
        wait_sent(relayed.at[pl.ds(0, 16)], side_send)


def ladder_of(amplitudes, integrals, tile_width):
    h = tile_width // 4
    count, depth = amplitudes.shape
    owned = integrals.shape[0]
    step = owned // 8
    f32 = jnp.float32
    bf16 = jnp.bfloat16
    dma = pltpu.SemaphoreType.DMA
    return pl.pallas_call(
        functools.partial(ladder_kernel, h),
        out_shape=pltpu.VMEM((count, tile_width * h), f32),
        in_specs=[pl.BlockSpec(memory_space=pl.ANY), pl.BlockSpec(memory_space=pl.ANY)],
        out_specs=pl.BlockSpec(memory_space=pltpu.VMEM),
        scratch_shapes=[
            pltpu.VMEM((count, depth), f32),
            pltpu.VMEM((2, step, depth), f32),
            pltpu.VMEM((owned, depth), bf16),
            pltpu.VMEM((owned, depth), bf16),
            pltpu.VMEM((3, count, depth), f32),
            pltpu.VMEM((8 * LANES, depth), bf16),
            pltpu.VMEM((2, h, 2, 2, h, 4 * LANES), f32),
            pltpu.VMEM((4, 2, h, 2, h, LANES), f32),
            pltpu.VMEM((3, 2 * h, 2, h, LANES), f32),
            pltpu.VMEM((4, 2 * h, 2, h, LANES), f32),
            pltpu.VMEM((32, h * h // 4, LANES), f32),
            pltpu.VMEM((32, h * h // 4, LANES), f32),
            pltpu.VMEM((32, h * h // 4, LANES), f32),
            pltpu.VMEM((32, h * h // 4, LANES), f32),
            pltpu.VMEM((32, h * h // 4, LANES), f32),
            pltpu.VMEM((2, 2, h * h, LANES), f32),
            pltpu.VMEM((2, h * h, LANES), f32),
            pltpu.VMEM((tile_width * h, LANES), f32),
            dma, dma((2,)), dma, dma((3, 4)),
            dma, dma((4, 2)), dma, dma((3, 2, 2)),
            dma, dma, dma((18,)), dma((18,)), dma, dma,
        ],
        compiler_params=pltpu.CompilerParams(
            collective_id=0, has_side_effects=True, vmem_limit_bytes=58 * 1024 * 1024
        ),
        name="ladder",
    )(amplitudes, integrals)


def block_body(amplitudes, integrals, eps_occ, eps_vir, pair_list):
    tile_width = eps_vir.shape[0] // 2
    first = lax.axis_index("virt") < lax.axis_size("virt") // 2
    sign = jnp.where(first, jnp.float32(1.0), jnp.float32(-1.0))
    raw = ladder_of(amplitudes, integrals, tile_width)
    raw, eps_occ, eps_vir, pair_list = lax.optimization_barrier(
        (raw, eps_occ, eps_vir, pair_list)
    )
    ladder = sign * raw
    return (ladder, updated(ladder, eps_occ, eps_vir, pair_list))


def solution(mesh):
    in_specs = (P("pair", "virt"), P("pair", "virt"), P(), P(), P("pair", None))
    out_specs = (P("pair", "virt"), P("pair", "virt"))
    fits = mesh.shape["pair"] == 4 and mesh.shape["virt"] == 8

    def body(amplitudes, integrals, eps_occ, eps_vir, pair_list):
        tiled = eps_vir.shape[0] % 64 == 0 and amplitudes.shape[0] <= LANES
        tiled = tiled and amplitudes.shape[1] % (12 * LANES) == 0
        chosen = block_body if fits and tiled else any_mesh_body
        return chosen(amplitudes, integrals, eps_occ, eps_vir, pair_list)

    return jax.shard_map(body, mesh=mesh, in_specs=in_specs, out_specs=out_specs, check_vma=False)
```
